32 devices in a mesh: gauss: 16 (over z, x, core), tile: 2 (over y).
Axes of the slice: x: 2, y: 2, z: 4, core: 2. Of those that a mesh axis runs over, the one named last changes fastest.
Arguments:
- splats: float32 [9, 32768], P(None, ('gauss', 'tile')), may hold values from -8 to 260, as said below
- sh_coeffs: float32 [48, 32768], P(None, ('gauss', 'tile')), may hold values from -2 to 2
- send_list: int32 [32768], P(('gauss', 'tile')), may hold values from 0 to 1023, as said below
- block_slots: int32 [16, 96, 128], P('gauss', 'tile'), may hold values from 0 to 1023, as said below
- block_tiles: int32 [16, 96], P('gauss', 'tile'), may hold values from 0 to 8, as said below
- target: float32 [3, 256, 256], P(None, 'gauss', 'tile'), may hold values from 0 to 1
Outputs:
- rendered: float32 [3, 256, 256], P(None, 'gauss', 'tile')
- grad_splats: float32 [9, 32768], P(None, ('gauss', 'tile'))
- grad_sh: float32 [48, 32768], P(None, ('gauss', 'tile'))
The draws below stay inside these ranges and needn't reach their ends.
Inputs may be any that keep to these rules, and one draw needn't show every extreme that they name: `send_list`: each device's 1024 entries are a permutation of 0 to 1023. `block_tiles`: each device's 48 entries never fall; each of its tiles 0 to 7 has at least one block; the value 8 marks an unused slot; in every draw some device uses all 48 slots. `block_slots`: entries index the device's received Gaussians. `splats`: conics are positive definite; view directions have unit length; opacity logits (row 5) lie between -8 and -2.
All inputs are finite; a program needn't handle non-finite values.
Results may differ from the reference program's by a relative error of at most 0.0003.
Values sent between devices are 32-bit elements; how exact they have to be, the bound alone decides.
A program may use at most 64 MiB of HBM per device.

```python
import math
import jax
import jax.numpy as jnp
from jax import lax

TILE_SIDE = 16
BLOCK_LEN = 128
SH_COEFFS = 48
TILES_DEV = 8
BLOCK_SLOTS = 48
SEND_CAP = 64
ROW_BANDS = 16
COL_BANDS = 2
OWN_SLOTS = 1024
GAUSSIANS = 32768
IMAGE_H = 256
IMAGE_W = 256


def owner_orders(key):
    devices_total = ROW_BANDS * COL_BANDS
    subkeys = jax.random.split(jax.random.fold_in(key, 11), devices_total)
    return jax.vmap(lambda single: jax.random.permutation(single, OWN_SLOTS))(subkeys).astype(jnp.int32)


def draw_send_list(key, part):
    return owner_orders(key).reshape(-1)


def draw_splats(key, part):
    orders = owner_orders(key)
    devices_total = ROW_BANDS * COL_BANDS
    position = jnp.arange(OWN_SLOTS)
    dest_band = position // SEND_CAP
    dest_tile = position % SEND_CAP % TILES_DEV
    col_band = jnp.arange(devices_total) % COL_BANDS
    subkeys = jax.random.split(jax.random.fold_in(key, 23), 8)
    grid_shape = (devices_total, OWN_SLOTS)
    scale_low, scale_high, logit_low, logit_high = (1.5, 5.0, -7.0, -2.0)
    offset_x = jax.random.uniform(subkeys[0], grid_shape, jnp.float32, -4.0, TILE_SIDE + 4.0)
    offset_y = jax.random.uniform(subkeys[1], grid_shape, jnp.float32, -4.0, TILE_SIDE + 4.0)
    place_x = (TILE_SIDE * (TILES_DEV * col_band[:, None] + dest_tile[None, :])).astype(jnp.float32) + offset_x
    place_y = (TILE_SIDE * dest_band[None, :] + 0 * col_band[:, None]).astype(jnp.float32) + offset_y
    scale_first = jnp.exp(jax.random.uniform(subkeys[2], grid_shape, jnp.float32, math.log(scale_low), math.log(scale_high)))
    scale_second = jnp.exp(jax.random.uniform(subkeys[3], grid_shape, jnp.float32, math.log(scale_low), math.log(scale_high)))
    angles = jax.random.uniform(subkeys[4], grid_shape, jnp.float32, -math.pi, math.pi)
    inverse_first = 1.0 / (scale_first * scale_first)
    inverse_second = 1.0 / (scale_second * scale_second)
    cosine = jnp.cos(angles)
    sine = jnp.sin(angles)
    conic_a = cosine * cosine * inverse_first + sine * sine * inverse_second
    conic_c = sine * sine * inverse_first + cosine * cosine * inverse_second
    conic_b = cosine * sine * (inverse_first - inverse_second)
    logits = jax.random.uniform(subkeys[5], grid_shape, jnp.float32, logit_low, logit_high)
    along_z = jax.random.uniform(subkeys[6], grid_shape, jnp.float32, 0.6, 1.0)
    azimuth = jax.random.uniform(subkeys[7], grid_shape, jnp.float32, -math.pi, math.pi)
    radial = jnp.sqrt(1.0 - along_z * along_z)
    values = jnp.stack([place_x, place_y, conic_a, conic_b, conic_c, logits, radial * jnp.cos(azimuth), radial * jnp.sin(azimuth), along_z])
    placed = jnp.zeros((9, devices_total, OWN_SLOTS), jnp.float32).at[:, jnp.arange(devices_total)[:, None], orders].set(values)
    return placed.reshape(9, devices_total * OWN_SLOTS)


def tile_layout(key):
    devices_total = ROW_BANDS * COL_BANDS
    subkeys = jax.random.split(jax.random.fold_in(key, 37), 4)
    base_live = jax.random.randint(subkeys[0], (devices_total,), TILES_DEV, 3 * TILES_DEV + 1)
    heavy = jax.random.randint(subkeys[1], (devices_total,), 0, 8) == 0
    forced = jax.random.randint(subkeys[2], (), 0, devices_total)
    live = jnp.where(heavy | (jnp.arange(devices_total) == forced), BLOCK_SLOTS, base_live)
    slot_pos = jnp.arange(BLOCK_SLOTS)
    extra = jax.random.randint(subkeys[3], (devices_total, BLOCK_SLOTS), 0, TILES_DEV)
    tiles_drawn = jnp.where(slot_pos[None, :] < TILES_DEV, slot_pos[None, :], extra)
    tiles_drawn = jnp.where(slot_pos[None, :] < live[:, None], tiles_drawn, TILES_DEV)
    return jnp.sort(tiles_drawn, axis=1).astype(jnp.int32)


def draw_block_tiles(key, part):
    return tile_layout(key).reshape(ROW_BANDS, COL_BANDS * BLOCK_SLOTS)


def draw_block_slots(key, part):
    devices_total = ROW_BANDS * COL_BANDS
    tiles_drawn = tile_layout(key)
    subkeys = jax.random.split(jax.random.fold_in(key, 41), 3)
    grid_shape = (devices_total, BLOCK_SLOTS, BLOCK_LEN)
    nearby = jnp.clip(tiles_drawn[:, :, None] + jax.random.randint(subkeys[0], grid_shape, -1, 2), 0, TILES_DEV - 1)
    source = jax.random.randint(subkeys[1], grid_shape, 0, ROW_BANDS)
    column = jax.random.randint(subkeys[2], grid_shape, 0, SEND_CAP // TILES_DEV)
    chosen = source * SEND_CAP + column * TILES_DEV + nearby
    return chosen.reshape(ROW_BANDS, COL_BANDS * BLOCK_SLOTS, BLOCK_LEN).astype(jnp.int32)


def block_levels(stream_key, dims, cuts, least, largest):
    def one(axis_at, parts):
        steps = jax.random.uniform(jax.random.fold_in(jax.random.fold_in(stream_key, 6), axis_at), (parts,), jnp.float32, least / len(cuts), largest / len(cuts))
        return jnp.repeat(jnp.exp(steps), dims[axis_at] // parts).reshape((-1,) + (1,) * (len(dims) - axis_at - 1))

    level = one(*cuts[0])
    for cut in cuts[1:]:
        level = level * one(*cut)
    return level


def scatter_about(own_key, shape, scale, limit, pieces=(), dtype=jnp.bfloat16):
    array = scale * jax.random.normal(own_key, shape, jnp.float32)
    if pieces:
        array = array * block_levels(own_key, shape, pieces, -0.22, 0.18)
    return jnp.clip(array, -limit, limit).astype(dtype)


def setup_inputs(seed: int = 0) -> dict:
    key_list = jax.random.split(jax.random.key(seed), 7)
    splats = draw_splats(jax.random.fold_in(key_list[6], 71), 0)
    sh_coeffs = scatter_about(key_list[1], (SH_COEFFS, GAUSSIANS), 0.35, 2.0, ((1, 32),), jnp.float32)
    send_list = draw_send_list(jax.random.fold_in(key_list[6], 71), 0)
    block_slots = draw_block_slots(jax.random.fold_in(key_list[6], 71), 0)
    block_tiles = draw_block_tiles(jax.random.fold_in(key_list[6], 71), 0)
    target = jnp.clip(1.0 * jax.random.uniform(key_list[5], (3, IMAGE_H, IMAGE_W), jnp.float32) ** block_levels(key_list[5], (3, IMAGE_H, IMAGE_W), ((1, 16), (2, 2)), -0.2, 0.2), 0.0, 1.0)
    return dict(splats=splats, sh_coeffs=sh_coeffs, send_list=send_list, block_slots=block_slots, block_tiles=block_tiles, target=target)


HIGHEST = lax.Precision.HIGHEST
BASE_ZERO = 0.28209479177387814
BASE_ONE = 0.4886025119029199
BASE_TWO = (1.0925484305920792, -1.0925484305920792, 0.31539156525252005, -1.0925484305920792, 0.5462742152960396)
BASE_THREE = (-0.5900435899266435, 2.890611442640554, -0.4570457994644658, 0.3731763325901154, -0.4570457994644658, 1.445305721320277, -0.5900435899266435)
CONST_ONE = 0.0001
CONST_TWO = 0.0009

def harmonics(direction):
    coord_x, coord_y, coord_z = (direction[0], direction[1], direction[2])
    square_x, square_y, square_z = (coord_x * coord_x, coord_y * coord_y, coord_z * coord_z)
    rows_list = [jnp.full_like(coord_x, BASE_ZERO), -BASE_ONE * coord_y, BASE_ONE * coord_z, -BASE_ONE * coord_x, BASE_TWO[0] * coord_x * coord_y, BASE_TWO[1] * coord_y * coord_z, BASE_TWO[2] * (2.0 * square_z - square_x - square_y), BASE_TWO[3] * coord_x * coord_z, BASE_TWO[4] * (square_x - square_y), BASE_THREE[0] * coord_y * (3.0 * square_x - square_y), BASE_THREE[1] * coord_x * coord_y * coord_z, BASE_THREE[2] * coord_y * (4.0 * square_z - square_x - square_y), BASE_THREE[3] * coord_z * (2.0 * square_z - 3.0 * square_x - 3.0 * square_y), BASE_THREE[4] * coord_x * (4.0 * square_z - square_x - square_y), BASE_THREE[5] * coord_z * (square_x - square_y), BASE_THREE[6] * coord_x * (square_x - 3.0 * square_y)]
    return jnp.stack(rows_list)

def shade(direction, coeffs):
    basis = harmonics(direction)
    return 0.5 + lax.optimization_barrier(jnp.sum(coeffs.reshape(3, 16, -1) * basis[None], axis=1))

def composite(records):
    members = records.shape[1]
    pixels = jnp.arange(TILE_SIDE * TILE_SIDE)
    pixel_u = (pixels % TILE_SIDE).astype(jnp.float32)
    pixel_v = (pixels // TILE_SIDE).astype(jnp.float32)
    delta_x = pixel_u[None, :] - records[0][:, None]
    delta_y = pixel_v[None, :] - records[1][:, None]
    exponent = -0.5 * (records[2][:, None] * delta_x * delta_x + records[4][:, None] * delta_y * delta_y) - records[3][:, None] * delta_x * delta_y
    alphas = jax.nn.sigmoid(records[5])[:, None] * jnp.exp(exponent)
    logged = jnp.log1p(-alphas)
    positions = jnp.arange(members)
    earlier_mask = (positions[None, :] < positions[:, None]).astype(jnp.float32)
    before = jnp.dot(earlier_mask, logged, precision=HIGHEST, preferred_element_type=jnp.float32)
    weight = alphas * jnp.exp(before)
    colour = jnp.dot(records[6:9], weight, precision=HIGHEST, preferred_element_type=jnp.float32)
    return jnp.concatenate([colour, lax.optimization_barrier(jnp.sum(logged, axis=0, keepdims=True))], axis=0)

def combine(results, tile_ids):
    positions = jnp.arange(results.shape[0])
    earlier = ((tile_ids[:, None] == tile_ids[None, :]) & (positions[None, :] < positions[:, None])).astype(jnp.float32)
    prefix = jnp.dot(earlier, results[:, 3], precision=HIGHEST, preferred_element_type=jnp.float32)
    member = (jnp.arange(TILES_DEV)[:, None] == tile_ids[None, :]).astype(jnp.float32)
    shaded = jnp.exp(prefix)[:, None, :] * results[:, 0:3]
    return jnp.einsum('kb,bcp->kcp', member, shaded, precision=HIGHEST)

def to_image(tiles_img):
    return tiles_img.reshape(TILES_DEV, 3, TILE_SIDE, TILE_SIDE).transpose(1, 2, 0, 3).reshape(3, TILE_SIDE, TILES_DEV * TILE_SIDE)

def window():
    tap_offsets = jnp.arange(11).astype(jnp.float32) - 5.0
    profile = jnp.exp(-tap_offsets * tap_offsets / 4.5)
    return profile / jnp.sum(profile)

def blur(padded, rows_out, cols_out):
    weights = window()
    across = weights[0] * padded[..., :, 0:cols_out]
    for offset in range(1, 11):
        across = across + weights[offset] * padded[..., :, offset:offset + cols_out]
    result = weights[0] * across[..., 0:rows_out, :]
    for offset in range(1, 11):
        result = result + weights[offset] * across[..., offset:offset + rows_out, :]
    return result

def similarity(mu_x, mu_y, sq_x, sq_y, cross_xy):
    mean_xy = mu_x * mu_y
    numerator = (2.0 * mean_xy + CONST_ONE) * (2.0 * (cross_xy - mean_xy) + CONST_TWO)
    denominator = (mu_x * mu_x + mu_y * mu_y + CONST_ONE) * (sq_x - mu_x * mu_x + sq_y - mu_y * mu_y + CONST_TWO)
    return numerator / denominator

def render(splats, sh_coeffs, send_list, block_slots, block_tiles):
    colour = shade(splats[6:9], sh_coeffs)
    records = jnp.concatenate([splats[0:6], colour], axis=0)
    slot_ids = jnp.arange(OWN_SLOTS).astype(jnp.int32)

    @jax.checkpoint
    def one_device(device):
        row_band = device // COL_BANDS
        col_band = device % COL_BANDS
        owner_ids = slot_ids // SEND_CAP * COL_BANDS + col_band
        chosen = owner_ids * OWN_SLOTS + send_list[owner_ids * OWN_SLOTS + row_band * SEND_CAP + slot_ids % SEND_CAP]
        received = records[:, chosen]
        tile_ids = lax.dynamic_slice_in_dim(block_tiles[row_band], (col_band * BLOCK_SLOTS).astype(jnp.int32), BLOCK_SLOTS, 0)
        slot_rows = lax.dynamic_slice_in_dim(block_slots[row_band], (col_band * BLOCK_SLOTS).astype(jnp.int32), BLOCK_SLOTS, 0)
        gathered = received[:, slot_rows.reshape(-1)].reshape(9, BLOCK_SLOTS, BLOCK_LEN)
        anchor_x = (TILE_SIDE * (TILES_DEV * col_band + jnp.minimum(tile_ids, TILES_DEV - 1))).astype(jnp.float32)
        anchor_y = (TILE_SIDE * row_band).astype(jnp.float32)
        shifted = jnp.concatenate([gathered[0:1] - anchor_x[None, :, None], gathered[1:2] - anchor_y, gathered[2:9]], axis=0)
        per_block = jnp.moveaxis(shifted, 1, 0)
        results = jax.vmap(composite)(per_block)
        return to_image(combine(results, tile_ids))
    pictures = lax.map(one_device, jnp.arange(ROW_BANDS * COL_BANDS).astype(jnp.int32))
    pictures = pictures.reshape(ROW_BANDS, COL_BANDS, 3, TILE_SIDE, TILES_DEV * TILE_SIDE)
    return pictures.transpose(2, 0, 3, 1, 4).reshape(3, IMAGE_H, IMAGE_W)

def loss_of(rendered, target):
    stacked = jnp.stack([rendered, target, rendered * rendered, target * target, rendered * target])
    padded = jnp.pad(stacked, ((0, 0), (0, 0), (5, 5), (5, 5)))
    moments = blur(padded, IMAGE_H, IMAGE_W)
    ssim = similarity(moments[0], moments[1], moments[2], moments[3], moments[4])
    residue = rendered - target
    return jnp.sum(0.8 * residue * residue) + jnp.sum(0.2 * (1.0 - ssim))

def reference(splats, sh_coeffs, send_list, block_slots, block_tiles, target):

    def objective(splat_rows, coeff_rows):
        rendered = render(splat_rows, coeff_rows, send_list, block_slots, block_tiles)
        return (loss_of(rendered, target), rendered)
    loss_value, pullback, rendered = jax.vjp(objective, splats, sh_coeffs, has_aux=True)
    grad_splats, grad_sh = pullback(jnp.ones_like(loss_value))
    return (rendered, grad_splats, grad_sh)
```

```python
import jax
import jax.numpy as jnp
from jax import lax
from jax.experimental import pallas as pl
from jax.experimental.pallas import tpu as pltpu
from jax.sharding import PartitionSpec as P

TILE_SIDE = 16
TILES_DEV = 8


HIGHEST = lax.Precision.HIGHEST
BASE_ZERO = 0.28209479177387814
BASE_ONE = 0.4886025119029199
BASE_TWO = (
    1.0925484305920792,
    -1.0925484305920792,
    0.31539156525252005,
    -1.0925484305920792,
    0.5462742152960396,
)
BASE_THREE = (
    -0.5900435899266435,
    2.890611442640554,
    -0.4570457994644658,
    0.3731763325901154,
    -0.4570457994644658,
    1.445305721320277,
    -0.5900435899266435,
)
CONST_ONE = 0.0001
CONST_TWO = 0.0009


def extended(cells, sides, width):
    for axis, dim in sides:
        count = lax.axis_size(axis)
        ends = count - 1
        head = lax.slice_in_dim(cells, 0, width, axis=dim)
        tail = lax.slice_in_dim(cells, cells.shape[dim] - width, cells.shape[dim], axis=dim)
        cells = jnp.concatenate(
            [
                lax.ppermute(tail, axis, [(i, (i + 1) % count) for i in range(ends)]),
                cells,
                lax.ppermute(head, axis, [((i + 1) % count, i) for i in range(ends)]),
            ],
            axis=dim,
        )
    return cells


def harmonics(direction):
    coord_x, coord_y, coord_z = (direction[0], direction[1], direction[2])
    square_x, square_y, square_z = (coord_x * coord_x, coord_y * coord_y, coord_z * coord_z)
    rows_list = [
        jnp.full_like(coord_x, BASE_ZERO),
        -BASE_ONE * coord_y,
        BASE_ONE * coord_z,
        -BASE_ONE * coord_x,
        BASE_TWO[0] * coord_x * coord_y,
        BASE_TWO[1] * coord_y * coord_z,
        BASE_TWO[2] * (2.0 * square_z - square_x - square_y),
        BASE_TWO[3] * coord_x * coord_z,
        BASE_TWO[4] * (square_x - square_y),
        BASE_THREE[0] * coord_y * (3.0 * square_x - square_y),
        BASE_THREE[1] * coord_x * coord_y * coord_z,
        BASE_THREE[2] * coord_y * (4.0 * square_z - square_x - square_y),
        BASE_THREE[3] * coord_z * (2.0 * square_z - 3.0 * square_x - 3.0 * square_y),
        BASE_THREE[4] * coord_x * (4.0 * square_z - square_x - square_y),
        BASE_THREE[5] * coord_z * (square_x - square_y),
        BASE_THREE[6] * coord_x * (square_x - 3.0 * square_y),
    ]
    return jnp.stack(rows_list)


def shade(direction, coeffs):
    basis = harmonics(direction)
    return 0.5 + jnp.sum(coeffs.reshape(3, 16, -1) * basis[None], axis=1)


SEGMENTS = 8
STEPS = 16
BLOCK = SEGMENTS * STEPS
HALF = 128
CENTRE = 7.5
CHUNK = 256


def selector(slots_row, base, rows):
    rows_at = lax.broadcasted_iota(jnp.int32, (rows, slots_row.shape[1]), 0) + base
    return jnp.where(rows_at == slots_row, 1.0, 0.0).astype(jnp.bfloat16)


def halves(value):
    high = value.astype(jnp.bfloat16)
    low = (value - high.astype(jnp.float32)).astype(jnp.bfloat16)
    return high, low


def pixel_axes():
    lanes = lax.broadcasted_iota(jnp.int32, (SEGMENTS, HALF), 1)
    along = (lanes % TILE_SIDE).astype(jnp.float32) - CENTRE
    down = (lanes // TILE_SIDE).astype(jnp.float32) - CENTRE
    return along, (down, down + float(HALF // TILE_SIDE))


def columns_of(col_ref, step):
    sub = col_ref[step * SEGMENTS : (step + 1) * SEGMENTS, :]
    return [jnp.broadcast_to(sub[:, k : k + 1], (SEGMENTS, HALF)) for k in range(9)]


def alphas_of(cols, along, down):
    delta_x = along - cols[0]
    delta_y = down - cols[1]
    exponent = cols[2] * delta_x * delta_x + delta_y * (cols[3] * delta_x + cols[4] * delta_y)
    return cols[5] * jnp.exp(exponent)


def forward_kernel(
    tile_ref, info_ref, recv_ref, slots_ref, image_ref, rec_ref, saved_ref, pad_ref, split_ref, col_ref
):
    live = info_ref[0]
    own = recv_ref.shape[1]
    pad_ref[...] = jnp.zeros_like(pad_ref)
    pad_ref[0:9, :] = recv_ref[...]
    whole = pad_ref[...]
    first = whole.astype(jnp.bfloat16)
    rest = whole - first.astype(jnp.float32)
    second = rest.astype(jnp.bfloat16)
    third = (rest - second.astype(jnp.float32)).astype(jnp.bfloat16)
    split_ref[0:16, :] = first
    split_ref[16:32, :] = second
    split_ref[32:48, :] = third
    row_at = lax.broadcasted_iota(jnp.int32, (16, BLOCK), 0)
    base_y = info_ref[2].astype(jnp.float32) + CENTRE

    def collect(pair, carry):
        slots_row = slots_ref[pl.ds(pair, 1), :]
        found = jnp.zeros((48, 2 * BLOCK), jnp.float32)
        for base in range(0, own, CHUNK):
            found = found + jnp.dot(
                split_ref[:, base : base + CHUNK],
                selector(slots_row, base, CHUNK),
                preferred_element_type=jnp.float32,
            )
        joined = found[0:16] + found[16:32] + found[32:48]
        for side in range(2):
            slot = 2 * pair + side
            rec = joined[:, side * BLOCK : (side + 1) * BLOCK]
            tile = jnp.minimum(tile_ref[slot], TILES_DEV - 1)
            base_x = (info_ref[1] + TILE_SIDE * tile).astype(jnp.float32) + CENTRE
            shift = jnp.where(row_at == 0, base_x, jnp.where(row_at == 1, base_y, 0.0))
            scale = jnp.where(
                row_at == 3, -1.0, jnp.where((row_at == 2) | (row_at == 4), -0.5, 1.0)
            )
            shown = jnp.where(row_at == 5, 1.0 / (1.0 + jnp.exp(-rec)), (rec - shift) * scale)
            rec_ref[slot] = shown
        return carry

    lax.fori_loop(0, (live + 1) // 2, collect, 0)
    along, downs = pixel_axes()
    seg_at = lax.broadcasted_iota(jnp.int32, (SEGMENTS, HALF), 0)

    def draw(slot, carry):
        tile = tile_ref[slot]
        fresh = (slot == 0) | (tile != tile_ref[jnp.maximum(slot - 1, 0)])
        col_ref[...] = jnp.transpose(rec_ref[slot])
        through = [jnp.ones((SEGMENTS, HALF), jnp.float32) for side in range(2)]
        sums = [[jnp.zeros((SEGMENTS, HALF), jnp.float32) for c in range(3)] for side in range(2)]
        for step in range(STEPS):
            cols = columns_of(col_ref, step)
            for side in range(2):
                weight = alphas_of(cols, along, downs[side]) * through[side]
                through[side] = through[side] - weight
                for c in range(3):
                    sums[side][c] = sums[side][c] + cols[6 + c] * weight
        after = []
        for side in range(2):
            start = jnp.where(fresh, 1.0, carry[side])
            running = through[side]
            for shift in (1, 2, 4):
                running = jnp.where(
                    seg_at >= shift, running * pltpu.roll(running, shift, 0), running
                )
            before = jnp.where(seg_at == 0, 1.0, pltpu.roll(running, 1, 0)) * start
            after.append(start * running[SEGMENTS - 1 : SEGMENTS])
            lanes = slice(side * HALF, (side + 1) * HALF)
            saved_ref[slot, 0, :, lanes] = before
            saved_ref[slot, 1, :, lanes] = through[side]
            for c in range(3):
                saved_ref[slot, 2 + c, :, lanes] = sums[side][c]
                shade_sum = jnp.sum(before * sums[side][c], axis=0, keepdims=True)
                held = jnp.where(fresh, 0.0, image_ref[tile, c : c + 1, lanes])
                image_ref[tile, c : c + 1, lanes] = held + shade_sum
        return tuple(after)

    ones = jnp.ones((1, HALF), jnp.float32)
    lax.fori_loop(0, live, draw, (ones, ones))


def backward_kernel(
    tile_ref, info_ref, rec_ref, saved_ref, grad_ref, slots_ref, out_ref,
    col_ref, weight_ref, pull_ref, block_ref, acc_ref,
):
    live = info_ref[0]
    own = out_ref.shape[1]
    slots_total = rec_ref.shape[0]
    block_ref[...] = jnp.zeros_like(block_ref)
    acc_ref[...] = jnp.zeros_like(acc_ref)
    along, downs = pixel_axes()
    seg_at = lax.broadcasted_iota(jnp.int32, (SEGMENTS, HALF), 0)
    rows16 = lax.broadcasted_iota(jnp.int32, (16, 2 * HALF), 0)
    pixels = lax.broadcasted_iota(jnp.int32, (16, 2 * HALF), 1)
    wide_u = (pixels % TILE_SIDE).astype(jnp.float32) - CENTRE
    wide_v = (pixels // TILE_SIDE).astype(jnp.float32) - CENTRE
    basis = jnp.zeros((16, 2 * HALF), jnp.float32)
    for at, term in enumerate(
        (jnp.ones_like(wide_u), wide_u, wide_v, wide_u * wide_u, wide_u * wide_v, wide_v * wide_v)
    ):
        basis = jnp.where(rows16 == at, term, basis)
    basis = basis.astype(jnp.bfloat16)
    across = (((1,), (1,)), ((), ()))

    def pull(turn, carry):
        slot = live - 1 - turn
        tile = tile_ref[slot]
        final = (turn == 0) | (tile != tile_ref[jnp.minimum(slot + 1, slots_total - 1)])
        rec = rec_ref[slot]
        col_ref[...] = jnp.transpose(rec)
        grads = grad_ref[tile]
        after = []
        behind = []
        through = []
        colour_g = []
        for side in range(2):
            lanes = slice(side * HALF, (side + 1) * HALF)
            start = jnp.where(final, 0.0, carry[side])
            tints = [jnp.broadcast_to(grads[c : c + 1, lanes], (SEGMENTS, HALF)) for c in range(3)]
            colour_g.append(tints)
            total = tints[0] * saved_ref[slot, 2, :, lanes]
            for c in (1, 2):
                total = total + tints[c] * saved_ref[slot, 2 + c, :, lanes]
            factor = saved_ref[slot, 1, :, lanes]
            for shift in (1, 2, 4):
                inside = seg_at < SEGMENTS - shift
                total = jnp.where(
                    inside, total + factor * pltpu.roll(total, SEGMENTS - shift, 0), total
                )
                factor = jnp.where(
                    inside, factor * pltpu.roll(factor, SEGMENTS - shift, 0), factor
                )
            entering = total + factor * start
            after.append(entering[0:1])
            behind.append(
                jnp.where(seg_at < SEGMENTS - 1, pltpu.roll(entering, SEGMENTS - 1, 0), start)
            )
            through.append(saved_ref[slot, 0, :, lanes])
        alphas = [[], []]
        weights = [[], []]
        for step in range(STEPS):
            cols = columns_of(col_ref, step)
            for side in range(2):
                alpha = alphas_of(cols, along, downs[side])
                weight = alpha * through[side]
                through[side] = through[side] - weight
                alphas[side].append(alpha)
                weights[side].append(weight)
                lanes = slice(side * HALF, (side + 1) * HALF)
                weight_ref[step * SEGMENTS : (step + 1) * SEGMENTS, lanes] = weight
        for step in reversed(range(STEPS)):
            cols = columns_of(col_ref, step)
            for side in range(2):
                lanes = slice(side * HALF, (side + 1) * HALF)
                tints = colour_g[side]
                lit = tints[0] * cols[6] + tints[1] * cols[7] + tints[2] * cols[8]
                gap = lit - behind[side]
                behind[side] = behind[side] + alphas[side][step] * gap
                pull_ref[step * SEGMENTS : (step + 1) * SEGMENTS, lanes] = (
                    weights[side][step] * gap
                )
        found = lax.dot_general(
            basis,
            jnp.concatenate(halves(pull_ref[...]), axis=0),
            across,
            preferred_element_type=jnp.float32,
        )
        moment = found[:, :BLOCK] + found[:, BLOCK:]
        painted = lax.dot_general(
            jnp.concatenate(halves(grads), axis=0),
            jnp.concatenate(halves(weight_ref[...]), axis=0),
            across,
            preferred_element_type=jnp.float32,
        )
        painted = painted[0:8] + painted[8:16]
        painted = painted[:, :BLOCK] + painted[:, BLOCK:]
        m_0, m_x, m_y, m_xx, m_xy, m_yy = [moment[k : k + 1] for k in range(6)]
        at_x, at_y, con_a, con_b, con_c, open_s = [rec[k : k + 1] for k in range(6)]
        h_x = m_x - at_x * m_0
        h_y = m_y - at_y * m_0
        h_xx = m_xx - 2.0 * at_x * m_x + at_x * at_x * m_0
        h_xy = m_xy - at_x * m_y - at_y * m_x + at_x * at_y * m_0
        h_yy = m_yy - 2.0 * at_y * m_y + at_y * at_y * m_0
        block_ref[slot, 0:1, :] = -2.0 * con_a * h_x - con_b * h_y
        block_ref[slot, 1:2, :] = -2.0 * con_c * h_y - con_b * h_x
        block_ref[slot, 2:3, :] = -0.5 * h_xx
        block_ref[slot, 3:4, :] = -h_xy
        block_ref[slot, 4:5, :] = -0.5 * h_yy
        block_ref[slot, 5:6, :] = (1.0 - open_s) * m_0
        block_ref[slot, 6:9, :] = painted[0:3]
        return tuple(after)

    zeros = jnp.zeros((1, HALF), jnp.float32)
    lax.fori_loop(0, live, pull, (zeros, zeros))

    def spread(pair, carry):
        slots_row = slots_ref[pl.ds(pair, 1), :]
        both = jnp.concatenate([block_ref[2 * pair], block_ref[2 * pair + 1]], axis=1)
        parts = jnp.concatenate(halves(both), axis=0)
        for base in range(0, own, CHUNK):
            lanes = slice(base, base + CHUNK)
            acc_ref[:, lanes] += lax.dot_general(
                parts, selector(slots_row, base, CHUNK), across, preferred_element_type=jnp.float32
            )
        return carry

    lax.fori_loop(0, (live + 1) // 2, spread, 0)
    out_ref[...] = acc_ref[0:9, :] + acc_ref[16:25, :]


def smem():
    return pl.BlockSpec(memory_space=pltpu.SMEM)


def vmem():
    return pl.BlockSpec(memory_space=pltpu.VMEM)


def draw_tiles(tile_ids, info, received, pairs, slots_total):
    own = received.shape[1]
    side = TILE_SIDE * TILE_SIDE
    return pl.pallas_call(
        forward_kernel,
        out_shape=(
            jax.ShapeDtypeStruct((TILES_DEV, 8, side), jnp.float32),
            jax.ShapeDtypeStruct((slots_total, 16, BLOCK), jnp.float32),
            jax.ShapeDtypeStruct((slots_total, 5, SEGMENTS, side), jnp.float32),
        ),
        in_specs=[smem(), smem(), vmem(), vmem()],
        out_specs=(vmem(), vmem(), vmem()),
        scratch_shapes=[
            pltpu.VMEM((16, own), jnp.float32),
            pltpu.VMEM((48, own), jnp.bfloat16),
            pltpu.VMEM((BLOCK, 16), jnp.float32),
        ],
        name="draw_tiles",
    )(tile_ids, info, received, pairs)


def pull_tiles(tile_ids, info, recs, saved, grads, pairs, own):
    slots_total = recs.shape[0]
    side = TILE_SIDE * TILE_SIDE
    return pl.pallas_call(
        backward_kernel,
        out_shape=jax.ShapeDtypeStruct((9, own), jnp.float32),
        in_specs=[smem(), smem(), vmem(), vmem(), vmem(), vmem()],
        out_specs=vmem(),
        scratch_shapes=[
            pltpu.VMEM((BLOCK, 16), jnp.float32),
            pltpu.VMEM((BLOCK, side), jnp.float32),
            pltpu.VMEM((BLOCK, side), jnp.float32),
            pltpu.VMEM((slots_total, 16, BLOCK), jnp.float32),
            pltpu.VMEM((32, own), jnp.float32),
        ],
        name="pull_tiles",
    )(tile_ids, info, recs, saved, grads, pairs)


def to_image(tiles_img):
    return (
        tiles_img.reshape(TILES_DEV, 3, TILE_SIDE, TILE_SIDE)
        .transpose(1, 2, 0, 3)
        .reshape(3, TILE_SIDE, TILES_DEV * TILE_SIDE)
    )


def window():
    tap_offsets = jnp.arange(11).astype(jnp.float32) - 5.0
    profile = jnp.exp(-tap_offsets * tap_offsets / 4.5)
    return profile / jnp.sum(profile)


def blur(padded, rows_out, cols_out):
    weights = window()
    across = weights[0] * padded[..., :, 0:cols_out]
    for offset in range(1, 11):
        across = across + weights[offset] * padded[..., :, offset : offset + cols_out]
    result = weights[0] * across[..., 0:rows_out, :]
    for offset in range(1, 11):
        result = result + weights[offset] * across[..., offset : offset + rows_out, :]
    return result


def similarity(mu_x, mu_y, sq_x, sq_y, cross_xy):
    mean_xy = mu_x * mu_y
    numerator = (2.0 * mean_xy + CONST_ONE) * (2.0 * (cross_xy - mean_xy) + CONST_TWO)
    denominator = (mu_x * mu_x + mu_y * mu_y + CONST_ONE) * (
        sq_x - mu_x * mu_x + sq_y - mu_y * mu_y + CONST_TWO
    )
    return numerator / denominator


def five_products(padded):
    return jnp.stack(
        [padded[0], padded[1], padded[0] * padded[0], padded[1] * padded[1], padded[0] * padded[1]]
    )


def similarity_grads(moments):

    def partial_loss(mean_x, square_x, product_xy):
        return jnp.sum(
            0.2 * (1.0 - similarity(mean_x, moments[1], square_x, moments[3], product_xy))
        )

    return jnp.stack(jax.grad(partial_loss, argnums=(0, 1, 2))(moments[0], moments[2], moments[4]))


def body(splats, sh_coeffs, send_list, block_slots, block_tiles, target):
    row_band = lax.axis_index("gauss")
    col_band = lax.axis_index("tile")
    owners = lax.axis_size("gauss")
    peers = lax.axis_size("tile")
    own_records = jnp.concatenate([splats[0:6], shade(splats[6:9], sh_coeffs)], axis=0)
    received = lax.all_to_all(
        own_records[:, send_list], "gauss", split_axis=1, concat_axis=1, tiled=True
    )
    tile_ids = block_tiles[0]
    slot_rows = block_slots[0]
    slots_total = slot_rows.shape[0]
    live = jnp.sum((tile_ids < TILES_DEV).astype(jnp.int32))
    pixel_count = TILE_SIDE * TILE_SIDE
    info = jnp.stack([live, TILE_SIDE * TILES_DEV * col_band, TILE_SIDE * row_band]).astype(jnp.int32)
    pairs = (
        slot_rows.reshape(slots_total, SEGMENTS, STEPS)
        .transpose(0, 2, 1)
        .reshape(slots_total // 2, 2 * BLOCK)
    )
    tiles_img, recs, saved = draw_tiles(tile_ids, info, received, pairs, slots_total)
    tiles_img = tiles_img[:, 0:3]
    rendered = to_image(tiles_img)
    rows_here = rendered.shape[1]
    cols_here = rendered.shape[2]
    padded = extended(jnp.stack([rendered, target]), (("gauss", 2), ("tile", 3)), 10)
    moments = blur(five_products(padded), rows_here + 10, cols_here + 10)
    grads_map = similarity_grads(moments)
    row_ids = row_band * rows_here - 5 + jnp.arange(rows_here + 10)
    col_ids = col_band * cols_here - 5 + jnp.arange(cols_here + 10)
    inside = ((row_ids >= 0) & (row_ids < rows_here * owners))[:, None] & (
        (col_ids >= 0) & (col_ids < cols_here * peers)
    )[None, :]
    spread = blur(grads_map * inside.astype(jnp.float32), rows_here, cols_here)
    pixel_grad = (
        spread[0] + 2.0 * rendered * spread[1] + target * spread[2] + 1.6 * (rendered - target)
    )
    tile_grad = (
        pixel_grad.reshape(3, TILE_SIDE, TILES_DEV, TILE_SIDE)
        .transpose(2, 0, 1, 3)
        .reshape(TILES_DEV, 3, pixel_count)
    )
    tile_grad = jnp.pad(tile_grad, ((0, 0), (0, 5), (0, 0)))
    table_grad = pull_tiles(tile_ids, info, recs, saved, tile_grad, pairs, received.shape[1])
    back_records = lax.all_to_all(table_grad, "gauss", split_axis=1, concat_axis=1, tiled=True)
    own_grad = jnp.zeros_like(own_records).at[:, send_list].set(back_records)
    unused_colour, shade_pull = jax.vjp(shade, splats[6:9], sh_coeffs)
    dir_grad, grad_sh = shade_pull(own_grad[6:9])
    grad_splats = jnp.concatenate([own_grad[0:6], dir_grad], axis=0)
    return (rendered, grad_splats, grad_sh)


def solution(mesh):
    in_specs = (
        P(None, ("gauss", "tile")),
        P(None, ("gauss", "tile")),
        P(("gauss", "tile")),
        P("gauss", "tile", None),
        P("gauss", "tile"),
        P(None, "gauss", "tile"),
    )
    out_specs = (P(None, "gauss", "tile"), P(None, ("gauss", "tile")), P(None, ("gauss", "tile")))
    return jax.shard_map(body, mesh=mesh, in_specs=in_specs, out_specs=out_specs, check_vma=False)
```

```python
import functools
import math

import jax
import jax.numpy as jnp
from jax import lax
from jax.experimental import pallas as pl
from jax.experimental.pallas import tpu as pltpu
from jax.sharding import PartitionSpec as P

TILE_SIDE = 16
TILES_DEV = 8


HIGHEST = lax.Precision.HIGHEST
BASE_ZERO = 0.28209479177387814
BASE_ONE = 0.4886025119029199
BASE_TWO = (
    1.0925484305920792,
    -1.0925484305920792,
    0.31539156525252005,
    -1.0925484305920792,
    0.5462742152960396,
)
BASE_THREE = (
    -0.5900435899266435,
    2.890611442640554,
    -0.4570457994644658,
    0.3731763325901154,
    -0.4570457994644658,
    1.445305721320277,
    -0.5900435899266435,
)
CONST_ONE = 0.0001
CONST_TWO = 0.0009


def harmonics(direction):
    coord_x, coord_y, coord_z = (direction[0], direction[1], direction[2])
    square_x, square_y, square_z = (coord_x * coord_x, coord_y * coord_y, coord_z * coord_z)
    rows_list = [
        jnp.full_like(coord_x, BASE_ZERO),
        -BASE_ONE * coord_y,
        BASE_ONE * coord_z,
        -BASE_ONE * coord_x,
        BASE_TWO[0] * coord_x * coord_y,
        BASE_TWO[1] * coord_y * coord_z,
        BASE_TWO[2] * (2.0 * square_z - square_x - square_y),
        BASE_TWO[3] * coord_x * coord_z,
        BASE_TWO[4] * (square_x - square_y),
        BASE_THREE[0] * coord_y * (3.0 * square_x - square_y),
        BASE_THREE[1] * coord_x * coord_y * coord_z,
        BASE_THREE[2] * coord_y * (4.0 * square_z - square_x - square_y),
        BASE_THREE[3] * coord_z * (2.0 * square_z - 3.0 * square_x - 3.0 * square_y),
        BASE_THREE[4] * coord_x * (4.0 * square_z - square_x - square_y),
        BASE_THREE[5] * coord_z * (square_x - square_y),
        BASE_THREE[6] * coord_x * (square_x - 3.0 * square_y),
    ]
    return jnp.stack(rows_list)


def shade(direction, coeffs):
    basis = harmonics(direction)
    return 0.5 + jnp.sum(coeffs.reshape(3, 16, -1) * basis[None], axis=1)


SEGMENTS = 8
STEPS = 16
BLOCK = SEGMENTS * STEPS
HALF = 128
CENTRE = 7.5
CHUNK = 256


def selector(slots_row, base, rows):
    rows_at = lax.broadcasted_iota(jnp.int32, (rows, slots_row.shape[1]), 0) + base
    return jnp.where(rows_at == slots_row, 1.0, 0.0).astype(jnp.bfloat16)


def halves(value):
    high = value.astype(jnp.bfloat16)
    low = (value - high.astype(jnp.float32)).astype(jnp.bfloat16)
    return high, low


def pixel_axes():
    lanes = lax.broadcasted_iota(jnp.int32, (SEGMENTS, HALF), 1)
    along = (lanes % TILE_SIDE).astype(jnp.float32) - CENTRE
    down = (lanes // TILE_SIDE).astype(jnp.float32) - CENTRE
    return along, (down, down + float(HALF // TILE_SIDE))


def columns_of(col_ref, step):
    sub = col_ref[step * SEGMENTS : (step + 1) * SEGMENTS, :]
    return [jnp.broadcast_to(sub[:, k : k + 1], (SEGMENTS, HALF)) for k in range(9)]


def alphas_of(cols, along, down):
    delta_x = along - cols[0]
    delta_y = down - cols[1]
    exponent = cols[2] * delta_x * delta_x + delta_y * (cols[3] * delta_x + cols[4] * delta_y)
    return cols[5] * jnp.exp(exponent)


def forward_kernel(
    tile_ref, info_ref, recv_ref, slots_ref, picture_ref, rec_ref, saved_ref,
    pad_ref, split_ref, col_ref, image_ref,
):
    live = info_ref[0]
    own = recv_ref.shape[1]
    pad_ref[...] = jnp.zeros_like(pad_ref)
    pad_ref[0:9, :] = recv_ref[...]
    whole = pad_ref[...]
    first = whole.astype(jnp.bfloat16)
    rest = whole - first.astype(jnp.float32)
    second = rest.astype(jnp.bfloat16)
    third = (rest - second.astype(jnp.float32)).astype(jnp.bfloat16)
    split_ref[0:16, :] = first
    split_ref[16:32, :] = second
    split_ref[32:48, :] = third
    row_at = lax.broadcasted_iota(jnp.int32, (16, BLOCK), 0)
    base_y = info_ref[2].astype(jnp.float32) + CENTRE

    def collect(pair, carry):
        slots_row = slots_ref[pl.ds(pair, 1), :]
        found = jnp.zeros((48, 2 * BLOCK), jnp.float32)
        for base in range(0, own, CHUNK):
            found = found + jnp.dot(
                split_ref[:, base : base + CHUNK],
                selector(slots_row, base, CHUNK),
                preferred_element_type=jnp.float32,
            )
        joined = found[0:16] + found[16:32] + found[32:48]
        for side in range(2):
            slot = 2 * pair + side
            rec = joined[:, side * BLOCK : (side + 1) * BLOCK]
            tile = jnp.minimum(tile_ref[slot], TILES_DEV - 1)
            base_x = (info_ref[1] + TILE_SIDE * tile).astype(jnp.float32) + CENTRE
            shift = jnp.where(row_at == 0, base_x, jnp.where(row_at == 1, base_y, 0.0))
            scale = jnp.where(
                row_at == 3, -1.0, jnp.where((row_at == 2) | (row_at == 4), -0.5, 1.0)
            )
            shown = jnp.where(row_at == 5, 1.0 / (1.0 + jnp.exp(-rec)), (rec - shift) * scale)
            rec_ref[slot] = shown
        return carry

    lax.fori_loop(0, (live + 1) // 2, collect, 0)
    along, downs = pixel_axes()
    seg_at = lax.broadcasted_iota(jnp.int32, (SEGMENTS, HALF), 0)

    def draw(slot, carry):
        tile = tile_ref[slot]
        fresh = (slot == 0) | (tile != tile_ref[jnp.maximum(slot - 1, 0)])
        col_ref[...] = jnp.transpose(rec_ref[slot])
        through = [jnp.ones((SEGMENTS, HALF), jnp.float32) for side in range(2)]
        sums = [[jnp.zeros((SEGMENTS, HALF), jnp.float32) for c in range(3)] for side in range(2)]
        for step in range(STEPS):
            cols = columns_of(col_ref, step)
            for side in range(2):
                weight = alphas_of(cols, along, downs[side]) * through[side]
                through[side] = through[side] - weight
                for c in range(3):
                    sums[side][c] = sums[side][c] + cols[6 + c] * weight
        after = []
        for side in range(2):
            start = jnp.where(fresh, 1.0, carry[side])
            running = through[side]
            for shift in (1, 2, 4):
                running = jnp.where(
                    seg_at >= shift, running * pltpu.roll(running, shift, 0), running
                )
            before = jnp.where(seg_at == 0, 1.0, pltpu.roll(running, 1, 0)) * start
            after.append(start * running[SEGMENTS - 1 : SEGMENTS])
            lanes = slice(side * HALF, (side + 1) * HALF)
            saved_ref[slot, 0, :, lanes] = before
            saved_ref[slot, 1, :, lanes] = through[side]
            for c in range(3):
                saved_ref[slot, 2 + c, :, lanes] = sums[side][c]
                shade_sum = jnp.sum(before * sums[side][c], axis=0, keepdims=True)
                held = jnp.where(fresh, 0.0, image_ref[tile, c : c + 1, lanes])
                image_ref[tile, c : c + 1, lanes] = held + shade_sum
        return tuple(after)

    ones = jnp.ones((1, HALF), jnp.float32)
    lax.fori_loop(0, live, draw, (ones, ones))
    lane_tile = lax.broadcasted_iota(jnp.int32, (SEGMENTS, HALF), 1) // TILE_SIDE
    for side in range(2):
        lanes = slice(side * HALF, (side + 1) * HALF)
        for c in range(3):
            shown = jnp.zeros((SEGMENTS, HALF), jnp.float32)
            for tile in range(TILES_DEV):
                row = jnp.broadcast_to(image_ref[tile, c : c + 1, lanes], (SEGMENTS, HALF))
                moved = pltpu.roll(row, TILE_SIDE * tile, 1) if tile else row
                for bit in (1, 2, 4):
                    moved = jnp.where(
                        (seg_at & bit) > 0, pltpu.roll(moved, HALF - TILE_SIDE * bit, 1), moved
                    )
                shown = jnp.where(lane_tile == tile, moved, shown)
            picture_ref[c, side * SEGMENTS : (side + 1) * SEGMENTS, :] = shown


def backward_kernel(
    tile_ref, info_ref, rec_ref, saved_ref, grad_ref, slots_ref, out_ref,
    col_ref, weight_ref, pull_ref, block_ref, acc_ref,
):
    live = info_ref[0]
    own = out_ref.shape[1]
    slots_total = rec_ref.shape[0]
    block_ref[...] = jnp.zeros_like(block_ref)
    acc_ref[...] = jnp.zeros_like(acc_ref)
    along, downs = pixel_axes()
    seg_at = lax.broadcasted_iota(jnp.int32, (SEGMENTS, HALF), 0)
    rows16 = lax.broadcasted_iota(jnp.int32, (16, 2 * HALF), 0)
    pixels = lax.broadcasted_iota(jnp.int32, (16, 2 * HALF), 1)
    wide_u = (pixels % TILE_SIDE).astype(jnp.float32) - CENTRE
    wide_v = (pixels // TILE_SIDE).astype(jnp.float32) - CENTRE
    basis = jnp.zeros((16, 2 * HALF), jnp.float32)
    for at, term in enumerate(
        (jnp.ones_like(wide_u), wide_u, wide_v, wide_u * wide_u, wide_u * wide_v, wide_v * wide_v)
    ):
        basis = jnp.where(rows16 == at, term, basis)
    basis = basis.astype(jnp.bfloat16)
    across = (((1,), (1,)), ((), ()))

    def pull(turn, carry):
        slot = live - 1 - turn
        tile = tile_ref[slot]
        final = (turn == 0) | (tile != tile_ref[jnp.minimum(slot + 1, slots_total - 1)])
        rec = rec_ref[slot]
        col_ref[...] = jnp.transpose(rec)
        grads = grad_ref[tile]
        after = []
        behind = []
        through = []
        colour_g = []
        for side in range(2):
            lanes = slice(side * HALF, (side + 1) * HALF)
            start = jnp.where(final, 0.0, carry[side])
            tints = [jnp.broadcast_to(grads[c : c + 1, lanes], (SEGMENTS, HALF)) for c in range(3)]
            colour_g.append(tints)
            total = tints[0] * saved_ref[slot, 2, :, lanes]
            for c in (1, 2):
                total = total + tints[c] * saved_ref[slot, 2 + c, :, lanes]
            factor = saved_ref[slot, 1, :, lanes]
            for shift in (1, 2, 4):
                inside = seg_at < SEGMENTS - shift
                total = jnp.where(
                    inside, total + factor * pltpu.roll(total, SEGMENTS - shift, 0), total
                )
                factor = jnp.where(
                    inside, factor * pltpu.roll(factor, SEGMENTS - shift, 0), factor
                )
            entering = total + factor * start
            after.append(entering[0:1])
            behind.append(
                jnp.where(seg_at < SEGMENTS - 1, pltpu.roll(entering, SEGMENTS - 1, 0), start)
            )
            through.append(saved_ref[slot, 0, :, lanes])
        alphas = [[], []]
        weights = [[], []]
        for step in range(STEPS):
            cols = columns_of(col_ref, step)
            for side in range(2):
                alpha = alphas_of(cols, along, downs[side])
                weight = alpha * through[side]
                through[side] = through[side] - weight
                alphas[side].append(alpha)
                weights[side].append(weight)
                lanes = slice(side * HALF, (side + 1) * HALF)
                weight_ref[step * SEGMENTS : (step + 1) * SEGMENTS, lanes] = weight
        for step in reversed(range(STEPS)):
            cols = columns_of(col_ref, step)
            for side in range(2):
                lanes = slice(side * HALF, (side + 1) * HALF)
                tints = colour_g[side]
                lit = tints[0] * cols[6] + tints[1] * cols[7] + tints[2] * cols[8]
                gap = lit - behind[side]
                behind[side] = behind[side] + alphas[side][step] * gap
                pull_ref[step * SEGMENTS : (step + 1) * SEGMENTS, lanes] = (
                    weights[side][step] * gap
                )
        found = lax.dot_general(
            basis,
            jnp.concatenate(halves(pull_ref[...]), axis=0),
            across,
            preferred_element_type=jnp.float32,
        )
        moment = found[:, :BLOCK] + found[:, BLOCK:]
        painted = lax.dot_general(
            jnp.concatenate(halves(grads), axis=0),
            jnp.concatenate(halves(weight_ref[...]), axis=0),
            across,
            preferred_element_type=jnp.float32,
        )
        painted = painted[0:8] + painted[8:16]
        painted = painted[:, :BLOCK] + painted[:, BLOCK:]
        m_0, m_x, m_y, m_xx, m_xy, m_yy = [moment[k : k + 1] for k in range(6)]
        at_x, at_y, con_a, con_b, con_c, open_s = [rec[k : k + 1] for k in range(6)]
        h_x = m_x - at_x * m_0
        h_y = m_y - at_y * m_0
        h_xx = m_xx - 2.0 * at_x * m_x + at_x * at_x * m_0
        h_xy = m_xy - at_x * m_y - at_y * m_x + at_x * at_y * m_0
        h_yy = m_yy - 2.0 * at_y * m_y + at_y * at_y * m_0
        block_ref[slot, 0:1, :] = -2.0 * con_a * h_x - con_b * h_y
        block_ref[slot, 1:2, :] = -2.0 * con_c * h_y - con_b * h_x
        block_ref[slot, 2:3, :] = -0.5 * h_xx
        block_ref[slot, 3:4, :] = -h_xy
        block_ref[slot, 4:5, :] = -0.5 * h_yy
        block_ref[slot, 5:6, :] = (1.0 - open_s) * m_0
        block_ref[slot, 6:9, :] = painted[0:3]
        return tuple(after)

    zeros = jnp.zeros((1, HALF), jnp.float32)
    lax.fori_loop(0, live, pull, (zeros, zeros))

    def spread(pair, carry):
        slots_row = slots_ref[pl.ds(pair, 1), :]
        both = jnp.concatenate([block_ref[2 * pair], block_ref[2 * pair + 1]], axis=1)
        parts = jnp.concatenate(halves(both), axis=0)
        for base in range(0, own, CHUNK):
            lanes = slice(base, base + CHUNK)
            acc_ref[:, lanes] += lax.dot_general(
                parts, selector(slots_row, base, CHUNK), across, preferred_element_type=jnp.float32
            )
        return carry

    lax.fori_loop(0, (live + 1) // 2, spread, 0)
    out_ref[...] = acc_ref[0:9, :] + acc_ref[16:25, :]


def smem():
    return pl.BlockSpec(memory_space=pltpu.SMEM)


def vmem():
    return pl.BlockSpec(memory_space=pltpu.VMEM)


def draw_tiles(tile_ids, info, received, pairs, slots_total):
    own = received.shape[1]
    side = TILE_SIDE * TILE_SIDE
    return pl.pallas_call(
        forward_kernel,
        out_shape=(
            jax.ShapeDtypeStruct((3, TILE_SIDE, TILES_DEV * TILE_SIDE), jnp.float32),
            jax.ShapeDtypeStruct((slots_total, 16, BLOCK), jnp.float32),
            jax.ShapeDtypeStruct((slots_total, 5, SEGMENTS, side), jnp.float32),
        ),
        in_specs=[smem(), smem(), vmem(), vmem()],
        out_specs=(vmem(), vmem(), vmem()),
        scratch_shapes=[
            pltpu.VMEM((16, own), jnp.float32),
            pltpu.VMEM((48, own), jnp.bfloat16),
            pltpu.VMEM((BLOCK, 16), jnp.float32),
            pltpu.VMEM((TILES_DEV, 8, side), jnp.float32),
        ],
        name="draw_tiles",
    )(tile_ids, info, received, pairs)


def pull_tiles(tile_ids, info, recs, saved, grads, pairs, own):
    slots_total = recs.shape[0]
    side = TILE_SIDE * TILE_SIDE
    return pl.pallas_call(
        backward_kernel,
        out_shape=jax.ShapeDtypeStruct((9, own), jnp.float32),
        in_specs=[smem(), smem(), vmem(), vmem(), vmem(), vmem()],
        out_specs=vmem(),
        scratch_shapes=[
            pltpu.VMEM((BLOCK, 16), jnp.float32),
            pltpu.VMEM((BLOCK, side), jnp.float32),
            pltpu.VMEM((BLOCK, side), jnp.float32),
            pltpu.VMEM((slots_total, 16, BLOCK), jnp.float32),
            pltpu.VMEM((32, own), jnp.float32),
        ],
        name="pull_tiles",
    )(tile_ids, info, recs, saved, grads, pairs)


WAYS = [(down, right) for down in (-1, 0, 1) for right in (-1, 0, 1) if (down, right) != (0, 0)]
NORM = sum(math.exp(-m * m / 4.5) for m in range(-5, 6))


def halo_kernel(bands, cols_total, shown_ref, target_ref, out_ref, send_sem, recv_sem):
    band = lax.axis_index("gauss")
    column = lax.axis_index("tile")
    rows, cols = shown_ref.shape[1:]
    out_ref[...] = jnp.zeros_like(out_ref)
    barrier = pltpu.get_barrier_semaphore()

    def exists(way):
        there_band = band + way[0]
        there_col = column + way[1]
        return (
            (there_band >= 0) & (there_band < bands) & (there_col >= 0) & (there_col < cols_total)
        )

    def copies(at):
        down, right = WAYS[at]
        landing = len(WAYS) - 1 - at
        return [
            pltpu.make_async_remote_copy(
                src_ref=source,
                dst_ref=out_ref.at[
                    pl.ds(3 * kind, 3), pl.ds(rows * (1 - down), rows), pl.ds(cols * (1 - right), cols)
                ],
                send_sem=send_sem.at[kind, at],
                recv_sem=recv_sem.at[kind, landing],
                device_id=(band + down, column + right),
                device_id_type=pl.DeviceIdType.MESH,
            )
            for kind, source in enumerate((shown_ref, target_ref))
        ]

    for at, way in enumerate(WAYS):

        @pl.when(exists(way))
        def _(way=way):
            pl.semaphore_signal(
                barrier,
                inc=1,
                device_id=(band + way[0], column + way[1]),
                device_id_type=pl.DeviceIdType.MESH,
            )

    peers = sum(exists(way).astype(jnp.int32) for way in WAYS)
    pl.semaphore_wait(barrier, peers)

    for at, way in enumerate(WAYS):

        @pl.when(exists(way))
        def _(at=at):
            for copy in copies(at):
                copy.start()

    out_ref[0:3, rows : 2 * rows, cols : 2 * cols] = shown_ref[...]
    out_ref[3:6, rows : 2 * rows, cols : 2 * cols] = target_ref[...]
    for at, way in enumerate(WAYS):

        @pl.when(exists(way))
        def _(at=at):
            for copy in copies(at):
                copy.wait_send()
            for kind, source in enumerate((shown_ref, target_ref)):
                pltpu.make_async_remote_copy(
                    src_ref=source,
                    dst_ref=out_ref.at[
                        pl.ds(3 * kind, 3),
                        pl.ds(rows * (1 + WAYS[at][0]), rows),
                        pl.ds(cols * (1 + WAYS[at][1]), cols),
                    ],
                    send_sem=send_sem.at[kind, at],
                    recv_sem=recv_sem.at[kind, at],
                    device_id=(band + WAYS[at][0], column + WAYS[at][1]),
                    device_id_type=pl.DeviceIdType.MESH,
                ).wait_recv()


def exchange(rendered, target):
    channels, rows, cols = rendered.shape
    return pl.pallas_call(
        functools.partial(halo_kernel, lax.axis_size("gauss"), lax.axis_size("tile")),
        out_shape=jax.ShapeDtypeStruct((2 * channels, 3 * rows, 3 * cols), jnp.float32),
        in_specs=[vmem(), vmem()],
        out_specs=vmem(),
        scratch_shapes=[
            pltpu.SemaphoreType.DMA((2, len(WAYS))),
            pltpu.SemaphoreType.DMA((2, len(WAYS))),
        ],
        compiler_params=pltpu.CompilerParams(collective_id=0, has_side_effects=True),
        name="halo",
    )(rendered, target)


def banded(shape, offset):
    gap = (
        lax.broadcasted_iota(jnp.int32, shape, 0) - lax.broadcasted_iota(jnp.int32, shape, 1) + offset
    ).astype(jnp.float32)
    return jnp.where(jnp.abs(gap) < 5.5, jnp.exp(gap * gap / -4.5) * (1.0 / NORM), 0.0)


def exact_dot(left, right):
    return jnp.dot(left, right, precision=HIGHEST, preferred_element_type=jnp.float32)


def ssim_kernel(place_ref, wide_ref, out_ref, stack_ref):
    tall, wide = wide_ref.shape[1:]
    rows, cols = tall // 3, wide // 3
    row_from, rows_mid = rows // 2, 2 * rows
    col_from, cols_mid = cols // 2, 2 * cols
    for c in range(3):
        pic = wide_ref[c]
        aim = wide_ref[3 + c]
        for kind, plane in enumerate((pic, aim, pic * pic + aim * aim, pic * aim)):
            at = 3 * kind + c
            stack_ref[at * tall : (at + 1) * tall, :] = plane
    across = exact_dot(stack_ref[...], banded((wide, cols_mid), -col_from))
    moments = exact_dot(
        banded((rows_mid, tall), row_from),
        jnp.concatenate([across[at * tall : (at + 1) * tall] for at in range(12)], axis=1),
    )
    row_at = place_ref[0] + row_from - rows + lax.broadcasted_iota(jnp.int32, (rows_mid, cols_mid), 0)
    col_at = place_ref[1] + col_from - cols + lax.broadcasted_iota(jnp.int32, (rows_mid, cols_mid), 1)
    inside = (row_at >= 0) & (row_at < place_ref[2]) & (col_at >= 0) & (col_at < place_ref[3])
    slopes = [None] * 9
    for c in range(3):
        mu_x, mu_y, squares, cross = [
            moments[:, (3 * kind + c) * cols_mid : (3 * kind + c + 1) * cols_mid] for kind in range(4)
        ]
        mean_xy = mu_x * mu_y
        mean_sq = mu_x * mu_x + mu_y * mu_y
        top_1 = 2.0 * mean_xy + CONST_ONE
        top_2 = 2.0 * (cross - mean_xy) + CONST_TWO
        low_1 = mean_sq + CONST_ONE
        low_2 = squares - mean_sq + CONST_TWO
        inverse = -0.2 / (low_1 * low_2)
        value = top_1 * top_2 * inverse
        value_1 = value * low_2 * inverse * -5.0
        value_2 = value * low_1 * inverse * -5.0
        slope_mean = 2.0 * mu_y * (top_2 - top_1) * inverse - 2.0 * mu_x * (value_1 - value_2)
        for kind, slope in enumerate((slope_mean, -value_2, 2.0 * top_1 * inverse)):
            slopes[3 * kind + c] = jnp.where(inside, slope, 0.0)
    down = exact_dot(
        banded((rows, rows_mid), rows - row_from), jnp.concatenate(slopes, axis=1)
    )
    spread = exact_dot(
        jnp.concatenate([down[:, at * cols_mid : (at + 1) * cols_mid] for at in range(9)], axis=0),
        banded((cols_mid, cols), col_from - cols),
    )
    lane_row = lax.broadcasted_iota(jnp.int32, (SEGMENTS, HALF), 1) // TILE_SIDE
    seg_at = lax.broadcasted_iota(jnp.int32, (SEGMENTS, HALF), 0)
    out_ref[...] = jnp.zeros_like(out_ref)
    for c in range(3):
        pic = wide_ref[c, rows : 2 * rows, cols : 2 * cols]
        aim = wide_ref[3 + c, rows : 2 * rows, cols : 2 * cols]
        parts = [spread[(3 * kind + c) * rows : (3 * kind + c + 1) * rows] for kind in range(3)]
        total = parts[0] + 2.0 * pic * parts[1] + aim * parts[2] + 1.6 * (pic - aim)
        for side in range(2):
            part = total[side * SEGMENTS : (side + 1) * SEGMENTS]
            skewed = pltpu.roll(part, 0, 1, stride=TILE_SIDE, stride_axis=0)
            for tile in range(TILES_DEV):
                moved = pltpu.roll(skewed, HALF - TILE_SIDE * tile, 1) if tile else skewed
                kept = jnp.where(lane_row == seg_at, moved, 0.0)
                out_ref[tile, c : c + 1, side * HALF : (side + 1) * HALF] = jnp.sum(
                    kept, axis=0, keepdims=True
                )


def ssim_pull(place, wide):
    return pl.pallas_call(
        ssim_kernel,
        out_shape=jax.ShapeDtypeStruct((TILES_DEV, 8, TILE_SIDE * TILE_SIDE), jnp.float32),
        in_specs=[smem(), vmem()],
        out_specs=vmem(),
        scratch_shapes=[pltpu.VMEM((12 * wide.shape[1], wide.shape[2]), jnp.float32)],
        name="ssim_pull",
    )(place, wide)


def body(splats, sh_coeffs, send_list, block_slots, block_tiles, target):
    row_band = lax.axis_index("gauss")
    col_band = lax.axis_index("tile")
    owners = lax.axis_size("gauss")
    peers = lax.axis_size("tile")
    own_records = jnp.concatenate([splats[0:6], shade(splats[6:9], sh_coeffs)], axis=0)
    received = lax.all_to_all(
        own_records[:, send_list], "gauss", split_axis=1, concat_axis=1, tiled=True
    )
    tile_ids = block_tiles[0]
    slot_rows = block_slots[0]
    slots_total = slot_rows.shape[0]
    live = jnp.sum((tile_ids < TILES_DEV).astype(jnp.int32))
    info = jnp.stack([live, TILE_SIDE * TILES_DEV * col_band, TILE_SIDE * row_band]).astype(jnp.int32)
    pairs = (
        slot_rows.reshape(slots_total, SEGMENTS, STEPS)
        .transpose(0, 2, 1)
        .reshape(slots_total // 2, 2 * BLOCK)
    )
    rendered, recs, saved = draw_tiles(tile_ids, info, received, pairs, slots_total)
    rows_here, cols_here = rendered.shape[1:]
    place = jnp.stack(
        [row_band * rows_here, col_band * cols_here, rows_here * owners, cols_here * peers]
    ).astype(jnp.int32)
    tile_grad = ssim_pull(place, exchange(rendered, target))
    table_grad = pull_tiles(tile_ids, info, recs, saved, tile_grad, pairs, received.shape[1])
    back_records = lax.all_to_all(table_grad, "gauss", split_axis=1, concat_axis=1, tiled=True)
    own_grad = jnp.zeros_like(own_records).at[:, send_list].set(back_records)
    unused_colour, shade_pull = jax.vjp(shade, splats[6:9], sh_coeffs)
    dir_grad, grad_sh = shade_pull(own_grad[6:9])
    grad_splats = jnp.concatenate([own_grad[0:6], dir_grad], axis=0)
    return (rendered, grad_splats, grad_sh)


def solution(mesh):
    in_specs = (
        P(None, ("gauss", "tile")),
        P(None, ("gauss", "tile")),
        P(("gauss", "tile")),
        P("gauss", "tile", None),
        P("gauss", "tile"),
        P(None, "gauss", "tile"),
    )
    out_specs = (P(None, "gauss", "tile"), P(None, ("gauss", "tile")), P(None, ("gauss", "tile")))
    return jax.shard_map(body, mesh=mesh, in_specs=in_specs, out_specs=out_specs, check_vma=False)
```

```python
import functools
import math

import jax
import jax.numpy as jnp
from jax import lax
from jax.experimental import pallas as pl
from jax.experimental.pallas import tpu as pltpu
from jax.sharding import PartitionSpec as P

TILE_SIDE = 16
TILES_DEV = 8


HIGHEST = lax.Precision.HIGHEST
BASE_ZERO = 0.28209479177387814
BASE_ONE = 0.4886025119029199
BASE_TWO = (
    1.0925484305920792,
    -1.0925484305920792,
    0.31539156525252005,
    -1.0925484305920792,
    0.5462742152960396,
)
BASE_THREE = (
    -0.5900435899266435,
    2.890611442640554,
    -0.4570457994644658,
    0.3731763325901154,
    -0.4570457994644658,
    1.445305721320277,
    -0.5900435899266435,
)
CONST_ONE = 0.0001
CONST_TWO = 0.0009


def harmonics(direction):
    coord_x, coord_y, coord_z = (direction[0], direction[1], direction[2])
    square_x, square_y, square_z = (coord_x * coord_x, coord_y * coord_y, coord_z * coord_z)
    rows_list = [
        jnp.full_like(coord_x, BASE_ZERO),
        -BASE_ONE * coord_y,
        BASE_ONE * coord_z,
        -BASE_ONE * coord_x,
        BASE_TWO[0] * coord_x * coord_y,
        BASE_TWO[1] * coord_y * coord_z,
        BASE_TWO[2] * (2.0 * square_z - square_x - square_y),
        BASE_TWO[3] * coord_x * coord_z,
        BASE_TWO[4] * (square_x - square_y),
        BASE_THREE[0] * coord_y * (3.0 * square_x - square_y),
        BASE_THREE[1] * coord_x * coord_y * coord_z,
        BASE_THREE[2] * coord_y * (4.0 * square_z - square_x - square_y),
        BASE_THREE[3] * coord_z * (2.0 * square_z - 3.0 * square_x - 3.0 * square_y),
        BASE_THREE[4] * coord_x * (4.0 * square_z - square_x - square_y),
        BASE_THREE[5] * coord_z * (square_x - square_y),
        BASE_THREE[6] * coord_x * (square_x - 3.0 * square_y),
    ]
    return jnp.stack(rows_list)


def shade(direction, coeffs):
    basis = harmonics(direction)
    return 0.5 + jnp.sum(coeffs.reshape(3, 16, -1) * basis[None], axis=1)


SEGMENTS = 8
STEPS = 16
BLOCK = SEGMENTS * STEPS
HALF = 128
CENTRE = 7.5
CHUNK = 256


def selector(slots_row, base, rows):
    rows_at = lax.broadcasted_iota(jnp.int32, (rows, slots_row.shape[1]), 0) + base
    return jnp.where(rows_at == slots_row, 1.0, 0.0).astype(jnp.bfloat16)


def halves(value):
    high = value.astype(jnp.bfloat16)
    low = (value - high.astype(jnp.float32)).astype(jnp.bfloat16)
    return high, low


def pixel_axes():
    lanes = lax.broadcasted_iota(jnp.int32, (SEGMENTS, HALF), 1)
    along = (lanes % TILE_SIDE).astype(jnp.float32) - CENTRE
    down = (lanes // TILE_SIDE).astype(jnp.float32) - CENTRE
    return along, (down, down + float(HALF // TILE_SIDE))


def thirds(value):
    first = value.astype(jnp.bfloat16)
    rest = value - first.astype(jnp.float32)
    second = rest.astype(jnp.bfloat16)
    third = (rest - second.astype(jnp.float32)).astype(jnp.bfloat16)
    return first, second, third


def fill_widener(wide_ref):
    rows_at = lax.broadcasted_iota(jnp.int32, wide_ref.shape, 0) % 16
    field_at = lax.broadcasted_iota(jnp.int32, wide_ref.shape, 1) // HALF
    wide_ref[...] = jnp.where(rows_at == field_at, 1.0, 0.0).astype(jnp.bfloat16)


def widen(rec, wide_ref, column_ref):
    column_ref[...] = lax.dot_general(
        jnp.concatenate(thirds(rec), axis=0),
        wide_ref[...],
        (((0,), (0,)), ((), ())),
        preferred_element_type=jnp.float32,
    )


def columns_of(col_ref, step):
    rows = slice(step * SEGMENTS, (step + 1) * SEGMENTS)
    return [col_ref[rows, k * HALF : (k + 1) * HALF] for k in range(9)]


def alphas_of(cols, along, down):
    delta_x = along - cols[0]
    delta_y = down - cols[1]
    exponent = cols[2] * delta_x * delta_x + delta_y * (cols[3] * delta_x + cols[4] * delta_y)
    return cols[5] * jnp.exp(exponent)


def forward_kernel(
    tile_ref, info_ref, recv_ref, slots_ref, picture_ref, rec_ref, saved_ref,
    pad_ref, split_ref, col_ref, image_ref, wide_ref,
):
    live = info_ref[0]
    own = recv_ref.shape[1]
    pad_ref[...] = jnp.zeros_like(pad_ref)
    pad_ref[0:9, :] = recv_ref[...]
    for at, part in enumerate(thirds(pad_ref[...])):
        split_ref[16 * at : 16 * (at + 1), :] = part
    fill_widener(wide_ref)
    row_at = lax.broadcasted_iota(jnp.int32, (16, BLOCK), 0)
    base_y = info_ref[2].astype(jnp.float32) + CENTRE

    def collect(pair, carry):
        slots_row = slots_ref[pl.ds(pair, 1), :]
        found = jnp.zeros((48, 2 * BLOCK), jnp.float32)
        for base in range(0, own, CHUNK):
            found = found + jnp.dot(
                split_ref[:, base : base + CHUNK],
                selector(slots_row, base, CHUNK),
                preferred_element_type=jnp.float32,
            )
        joined = found[0:16] + found[16:32] + found[32:48]
        for side in range(2):
            slot = 2 * pair + side
            rec = joined[:, side * BLOCK : (side + 1) * BLOCK]
            tile = jnp.minimum(tile_ref[slot], TILES_DEV - 1)
            base_x = (info_ref[1] + TILE_SIDE * tile).astype(jnp.float32) + CENTRE
            shift = jnp.where(row_at == 0, base_x, jnp.where(row_at == 1, base_y, 0.0))
            scale = jnp.where(
                row_at == 3, -1.0, jnp.where((row_at == 2) | (row_at == 4), -0.5, 1.0)
            )
            shown = jnp.where(row_at == 5, 1.0 / (1.0 + jnp.exp(-rec)), (rec - shift) * scale)
            rec_ref[slot] = shown
        return carry

    lax.fori_loop(0, (live + 1) // 2, collect, 0)
    along, downs = pixel_axes()
    seg_at = lax.broadcasted_iota(jnp.int32, (SEGMENTS, HALF), 0)

    def draw_local(slot, column_ref):
        widen(rec_ref[slot], wide_ref, column_ref)
        through = [jnp.ones((SEGMENTS, HALF), jnp.float32) for side in range(2)]
        sums = [[jnp.zeros((SEGMENTS, HALF), jnp.float32) for c in range(3)] for side in range(2)]
        for step in range(STEPS):
            cols = columns_of(column_ref, step)
            for side in range(2):
                weight = alphas_of(cols, along, downs[side]) * through[side]
                through[side] = through[side] - weight
                for c in range(3):
                    sums[side][c] = sums[side][c] + cols[6 + c] * weight
        return through, sums

    def draw_join(slot, carry, through, sums):
        tile = tile_ref[slot]
        fresh = (slot == 0) | (tile != tile_ref[jnp.maximum(slot - 1, 0)])
        after = []
        for side in range(2):
            start = jnp.where(fresh, 1.0, carry[side])
            running = through[side]
            for shift in (1, 2, 4):
                running = jnp.where(
                    seg_at >= shift, running * pltpu.roll(running, shift, 0), running
                )
            before = jnp.where(seg_at == 0, 1.0, pltpu.roll(running, 1, 0)) * start
            after.append(start * running[SEGMENTS - 1 : SEGMENTS])
            lanes = slice(side * HALF, (side + 1) * HALF)
            saved_ref[slot, 0, :, lanes] = before
            saved_ref[slot, 1, :, lanes] = through[side]
            for c in range(3):
                saved_ref[slot, 2 + c, :, lanes] = sums[side][c]
                shade_sum = jnp.sum(before * sums[side][c], axis=0, keepdims=True)
                held = jnp.where(fresh, 0.0, image_ref[tile, c : c + 1, lanes])
                image_ref[tile, c : c + 1, lanes] = held + shade_sum
        return tuple(after)

    def draw(pair, carry):
        locals_two = [draw_local(2 * pair + k, col_ref.at[k]) for k in range(2)]
        for k in range(2):
            carry = draw_join(2 * pair + k, carry, *locals_two[k])
        return carry

    ones = jnp.ones((1, HALF), jnp.float32)
    lax.fori_loop(0, (live + 1) // 2, draw, (ones, ones))
    lane_tile = lax.broadcasted_iota(jnp.int32, (SEGMENTS, HALF), 1) // TILE_SIDE
    for side in range(2):
        lanes = slice(side * HALF, (side + 1) * HALF)
        for c in range(3):
            shown = jnp.zeros((SEGMENTS, HALF), jnp.float32)
            for tile in range(TILES_DEV):
                row = jnp.broadcast_to(image_ref[tile, c : c + 1, lanes], (SEGMENTS, HALF))
                moved = pltpu.roll(row, TILE_SIDE * tile, 1) if tile else row
                for bit in (1, 2, 4):
                    moved = jnp.where(
                        (seg_at & bit) > 0, pltpu.roll(moved, HALF - TILE_SIDE * bit, 1), moved
                    )
                shown = jnp.where(lane_tile == tile, moved, shown)
            picture_ref[c, side * SEGMENTS : (side + 1) * SEGMENTS, :] = shown


def backward_kernel(
    tile_ref, info_ref, rec_ref, saved_ref, grad_ref, slots_ref, out_ref,
    col_ref, weight_ref, pull_ref, block_ref, acc_ref, wide_ref,
):
    live = info_ref[0]
    own = out_ref.shape[1]
    slots_total = rec_ref.shape[0]
    block_ref[...] = jnp.zeros_like(block_ref)
    acc_ref[...] = jnp.zeros_like(acc_ref)
    fill_widener(wide_ref)
    along, downs = pixel_axes()
    seg_at = lax.broadcasted_iota(jnp.int32, (SEGMENTS, HALF), 0)
    rows16 = lax.broadcasted_iota(jnp.int32, (16, 2 * HALF), 0)
    pixels = lax.broadcasted_iota(jnp.int32, (16, 2 * HALF), 1)
    wide_u = (pixels % TILE_SIDE).astype(jnp.float32) - CENTRE
    wide_v = (pixels // TILE_SIDE).astype(jnp.float32) - CENTRE
    basis = jnp.zeros((16, 2 * HALF), jnp.float32)
    for at, term in enumerate(
        (jnp.ones_like(wide_u), wide_u, wide_v, wide_u * wide_u, wide_u * wide_v, wide_v * wide_v)
    ):
        basis = jnp.where(rows16 == at, term, basis)
    basis = basis.astype(jnp.bfloat16)
    across = (((1,), (1,)), ((), ()))

    def pull_one(slot, carry, column_ref, heavy_ref, force_ref):
        tile = tile_ref[slot]
        used = tile < TILES_DEV
        final = (slot >= live - 1) | (tile != tile_ref[jnp.minimum(slot + 1, slots_total - 1)])
        rec = rec_ref[slot]
        widen(rec, wide_ref, column_ref)
        grads = grad_ref[jnp.minimum(tile, TILES_DEV - 1)]
        after = []
        behind = []
        through = []
        colour_g = []
        for side in range(2):
            lanes = slice(side * HALF, (side + 1) * HALF)
            start = jnp.where(final, 0.0, carry[side])
            tints = [jnp.broadcast_to(grads[c : c + 1, lanes], (SEGMENTS, HALF)) for c in range(3)]
            colour_g.append(tints)
            total = tints[0] * saved_ref[slot, 2, :, lanes]
            for c in (1, 2):
                total = total + tints[c] * saved_ref[slot, 2 + c, :, lanes]
            factor = saved_ref[slot, 1, :, lanes]
            for shift in (1, 2, 4):
                inside = seg_at < SEGMENTS - shift
                total = jnp.where(
                    inside, total + factor * pltpu.roll(total, SEGMENTS - shift, 0), total
                )
                factor = jnp.where(
                    inside, factor * pltpu.roll(factor, SEGMENTS - shift, 0), factor
                )
            entering = total + factor * start
            after.append(entering[0:1])
            behind.append(
                jnp.where(seg_at < SEGMENTS - 1, pltpu.roll(entering, SEGMENTS - 1, 0), start)
            )
            through.append(saved_ref[slot, 0, :, lanes])
        alphas = [[], []]
        weights = [[], []]
        for step in range(STEPS):
            cols = columns_of(column_ref, step)
            for side in range(2):
                alpha = alphas_of(cols, along, downs[side])
                weight = alpha * through[side]
                through[side] = through[side] - weight
                alphas[side].append(alpha)
                weights[side].append(weight)
                lanes = slice(side * HALF, (side + 1) * HALF)
                heavy_ref[step * SEGMENTS : (step + 1) * SEGMENTS, lanes] = weight
        for step in reversed(range(STEPS)):
            cols = columns_of(column_ref, step)
            for side in range(2):
                lanes = slice(side * HALF, (side + 1) * HALF)
                tints = colour_g[side]
                lit = tints[0] * cols[6] + tints[1] * cols[7] + tints[2] * cols[8]
                gap = lit - behind[side]
                behind[side] = behind[side] + alphas[side][step] * gap
                force_ref[step * SEGMENTS : (step + 1) * SEGMENTS, lanes] = (
                    weights[side][step] * gap
                )
        found = lax.dot_general(
            basis,
            jnp.concatenate(halves(force_ref[...]), axis=0),
            across,
            preferred_element_type=jnp.float32,
        )
        moment = found[:, :BLOCK] + found[:, BLOCK:]
        painted = lax.dot_general(
            jnp.concatenate(halves(grads), axis=0),
            jnp.concatenate(halves(heavy_ref[...]), axis=0),
            across,
            preferred_element_type=jnp.float32,
        )
        painted = painted[0:8] + painted[8:16]
        painted = painted[:, :BLOCK] + painted[:, BLOCK:]
        m_0, m_x, m_y, m_xx, m_xy, m_yy = [moment[k : k + 1] for k in range(6)]
        at_x, at_y, con_a, con_b, con_c, open_s = [rec[k : k + 1] for k in range(6)]
        h_x = m_x - at_x * m_0
        h_y = m_y - at_y * m_0
        h_xx = m_xx - 2.0 * at_x * m_x + at_x * at_x * m_0
        h_xy = m_xy - at_x * m_y - at_y * m_x + at_x * at_y * m_0
        h_yy = m_yy - 2.0 * at_y * m_y + at_y * at_y * m_0
        block_ref[slot, 0:1, :] = jnp.where(used, -2.0 * con_a * h_x - con_b * h_y, 0.0)
        block_ref[slot, 1:2, :] = jnp.where(used, -2.0 * con_c * h_y - con_b * h_x, 0.0)
        block_ref[slot, 2:3, :] = jnp.where(used, -0.5 * h_xx, 0.0)
        block_ref[slot, 3:4, :] = jnp.where(used, -h_xy, 0.0)
        block_ref[slot, 4:5, :] = jnp.where(used, -0.5 * h_yy, 0.0)
        block_ref[slot, 5:6, :] = jnp.where(used, (1.0 - open_s) * m_0, 0.0)
        block_ref[slot, 6:9, :] = jnp.where(used, painted[0:3], 0.0)
        return tuple(after)

    def pull(turn, carry):
        pair = (live + 1) // 2 - 1 - turn
        for k in (1, 0):
            carry = pull_one(2 * pair + k, carry, col_ref.at[k], weight_ref.at[k], pull_ref.at[k])
        return carry

    zeros = jnp.zeros((1, HALF), jnp.float32)
    lax.fori_loop(0, (live + 1) // 2, pull, (zeros, zeros))

    def spread(pair, carry):
        slots_row = slots_ref[pl.ds(pair, 1), :]
        both = jnp.concatenate([block_ref[2 * pair], block_ref[2 * pair + 1]], axis=1)
        parts = jnp.concatenate(halves(both), axis=0)
        for base in range(0, own, CHUNK):
            lanes = slice(base, base + CHUNK)
            acc_ref[:, lanes] += lax.dot_general(
                parts, selector(slots_row, base, CHUNK), across, preferred_element_type=jnp.float32
            )
        return carry

    lax.fori_loop(0, (live + 1) // 2, spread, 0)
    out_ref[...] = acc_ref[0:9, :] + acc_ref[16:25, :]


def smem():
    return pl.BlockSpec(memory_space=pltpu.SMEM)


def vmem():
    return pl.BlockSpec(memory_space=pltpu.VMEM)


def draw_tiles(tile_ids, info, received, pairs, slots_total):
    own = received.shape[1]
    side = TILE_SIDE * TILE_SIDE
    return pl.pallas_call(
        forward_kernel,
        out_shape=(
            jax.ShapeDtypeStruct((3, TILE_SIDE, TILES_DEV * TILE_SIDE), jnp.float32),
            jax.ShapeDtypeStruct((slots_total, 16, BLOCK), jnp.float32),
            jax.ShapeDtypeStruct((slots_total, 5, SEGMENTS, side), jnp.float32),
        ),
        in_specs=[smem(), smem(), vmem(), vmem()],
        out_specs=(vmem(), vmem(), vmem()),
        scratch_shapes=[
            pltpu.VMEM((16, own), jnp.float32),
            pltpu.VMEM((48, own), jnp.bfloat16),
            pltpu.VMEM((2, BLOCK, 9 * HALF), jnp.float32),
            pltpu.VMEM((TILES_DEV + 1, 8, side), jnp.float32),
            pltpu.VMEM((48, 9 * HALF), jnp.bfloat16),
        ],
        name="draw_tiles",
    )(tile_ids, info, received, pairs)


def pull_tiles(tile_ids, info, recs, saved, grads, pairs, own):
    slots_total = recs.shape[0]
    side = TILE_SIDE * TILE_SIDE
    return pl.pallas_call(
        backward_kernel,
        out_shape=jax.ShapeDtypeStruct((9, own), jnp.float32),
        in_specs=[smem(), smem(), vmem(), vmem(), vmem(), vmem()],
        out_specs=vmem(),
        scratch_shapes=[
            pltpu.VMEM((2, BLOCK, 9 * HALF), jnp.float32),
            pltpu.VMEM((2, BLOCK, side), jnp.float32),
            pltpu.VMEM((2, BLOCK, side), jnp.float32),
            pltpu.VMEM((slots_total, 16, BLOCK), jnp.float32),
            pltpu.VMEM((32, own), jnp.float32),
            pltpu.VMEM((48, 9 * HALF), jnp.bfloat16),
        ],
        name="pull_tiles",
    )(tile_ids, info, recs, saved, grads, pairs)


WAYS = [(down, right) for down in (-1, 0, 1) for right in (-1, 0, 1) if (down, right) != (0, 0)]
NORM = sum(math.exp(-m * m / 4.5) for m in range(-5, 6))


def halo_kernel(bands, cols_total, shown_ref, target_ref, out_ref, send_sem, recv_sem):
    band = lax.axis_index("gauss")
    column = lax.axis_index("tile")
    rows, cols = shown_ref.shape[1:]
    out_ref[...] = jnp.zeros_like(out_ref)
    barrier = pltpu.get_barrier_semaphore()

    def exists(way):
        there_band = band + way[0]
        there_col = column + way[1]
        return (
            (there_band >= 0) & (there_band < bands) & (there_col >= 0) & (there_col < cols_total)
        )

    def copies(at):
        down, right = WAYS[at]
        landing = len(WAYS) - 1 - at
        return [
            pltpu.make_async_remote_copy(
                src_ref=source,
                dst_ref=out_ref.at[
                    pl.ds(3 * kind, 3), pl.ds(rows * (1 - down), rows), pl.ds(cols * (1 - right), cols)
                ],
                send_sem=send_sem.at[kind, at],
                recv_sem=recv_sem.at[kind, landing],
                device_id=(band + down, column + right),
                device_id_type=pl.DeviceIdType.MESH,
            )
            for kind, source in enumerate((shown_ref, target_ref))
        ]

    for at, way in enumerate(WAYS):

        @pl.when(exists(way))
        def _(way=way):
            pl.semaphore_signal(
                barrier,
                inc=1,
                device_id=(band + way[0], column + way[1]),
                device_id_type=pl.DeviceIdType.MESH,
            )

    peers = sum(exists(way).astype(jnp.int32) for way in WAYS)
    pl.semaphore_wait(barrier, peers)

    for at, way in enumerate(WAYS):

        @pl.when(exists(way))
        def _(at=at):
            for copy in copies(at):
                copy.start()

    out_ref[0:3, rows : 2 * rows, cols : 2 * cols] = shown_ref[...]
    out_ref[3:6, rows : 2 * rows, cols : 2 * cols] = target_ref[...]
    for at, way in enumerate(WAYS):

        @pl.when(exists(way))
        def _(at=at):
            for copy in copies(at):
                copy.wait_send()
            for kind, source in enumerate((shown_ref, target_ref)):
                pltpu.make_async_remote_copy(
                    src_ref=source,
                    dst_ref=out_ref.at[
                        pl.ds(3 * kind, 3),
                        pl.ds(rows * (1 + WAYS[at][0]), rows),
                        pl.ds(cols * (1 + WAYS[at][1]), cols),
                    ],
                    send_sem=send_sem.at[kind, at],
                    recv_sem=recv_sem.at[kind, at],
                    device_id=(band + WAYS[at][0], column + WAYS[at][1]),
                    device_id_type=pl.DeviceIdType.MESH,
                ).wait_recv()


def exchange(rendered, target):
    channels, rows, cols = rendered.shape
    return pl.pallas_call(
        functools.partial(halo_kernel, lax.axis_size("gauss"), lax.axis_size("tile")),
        out_shape=jax.ShapeDtypeStruct((2 * channels, 3 * rows, 3 * cols), jnp.float32),
        in_specs=[vmem(), vmem()],
        out_specs=vmem(),
        scratch_shapes=[
            pltpu.SemaphoreType.DMA((2, len(WAYS))),
            pltpu.SemaphoreType.DMA((2, len(WAYS))),
        ],
        compiler_params=pltpu.CompilerParams(collective_id=0, has_side_effects=True),
        name="halo",
    )(rendered, target)


def banded(shape, offset):
    gap = (
        lax.broadcasted_iota(jnp.int32, shape, 0) - lax.broadcasted_iota(jnp.int32, shape, 1) + offset
    ).astype(jnp.float32)
    return jnp.where(jnp.abs(gap) < 5.5, jnp.exp(gap * gap / -4.5) * (1.0 / NORM), 0.0)


def exact_dot(left, right):
    return jnp.dot(left, right, precision=HIGHEST, preferred_element_type=jnp.float32)


def ssim_kernel(place_ref, wide_ref, out_ref, stack_ref):
    tall, wide = wide_ref.shape[1:]
    rows, cols = tall // 3, wide // 3
    row_from, rows_mid = rows // 2, 2 * rows
    col_from, cols_mid = cols // 2, 2 * cols
    for c in range(3):
        pic = wide_ref[c]
        aim = wide_ref[3 + c]
        for kind, plane in enumerate((pic, aim, pic * pic + aim * aim, pic * aim)):
            at = 3 * kind + c
            stack_ref[at * tall : (at + 1) * tall, :] = plane
    across = exact_dot(stack_ref[...], banded((wide, cols_mid), -col_from))
    moments = exact_dot(
        banded((rows_mid, tall), row_from),
        jnp.concatenate([across[at * tall : (at + 1) * tall] for at in range(12)], axis=1),
    )
    row_at = place_ref[0] + row_from - rows + lax.broadcasted_iota(jnp.int32, (rows_mid, cols_mid), 0)
    col_at = place_ref[1] + col_from - cols + lax.broadcasted_iota(jnp.int32, (rows_mid, cols_mid), 1)
    inside = (row_at >= 0) & (row_at < place_ref[2]) & (col_at >= 0) & (col_at < place_ref[3])
    slopes = [None] * 9
    for c in range(3):
        mu_x, mu_y, squares, cross = [
            moments[:, (3 * kind + c) * cols_mid : (3 * kind + c + 1) * cols_mid] for kind in range(4)
        ]
        mean_xy = mu_x * mu_y
        mean_sq = mu_x * mu_x + mu_y * mu_y
        top_1 = 2.0 * mean_xy + CONST_ONE
        top_2 = 2.0 * (cross - mean_xy) + CONST_TWO
        low_1 = mean_sq + CONST_ONE
        low_2 = squares - mean_sq + CONST_TWO
        inverse = -0.2 / (low_1 * low_2)
        value = top_1 * top_2 * inverse
        value_1 = value * low_2 * inverse * -5.0
        value_2 = value * low_1 * inverse * -5.0
        slope_mean = 2.0 * mu_y * (top_2 - top_1) * inverse - 2.0 * mu_x * (value_1 - value_2)
        for kind, slope in enumerate((slope_mean, -value_2, 2.0 * top_1 * inverse)):
            slopes[3 * kind + c] = jnp.where(inside, slope, 0.0)
    down = exact_dot(
        banded((rows, rows_mid), rows - row_from), jnp.concatenate(slopes, axis=1)
    )
    spread = exact_dot(
        jnp.concatenate([down[:, at * cols_mid : (at + 1) * cols_mid] for at in range(9)], axis=0),
        banded((cols_mid, cols), col_from - cols),
    )
    lane_row = lax.broadcasted_iota(jnp.int32, (SEGMENTS, HALF), 1) // TILE_SIDE
    seg_at = lax.broadcasted_iota(jnp.int32, (SEGMENTS, HALF), 0)
    out_ref[...] = jnp.zeros_like(out_ref)
    for c in range(3):
        pic = wide_ref[c, rows : 2 * rows, cols : 2 * cols]
        aim = wide_ref[3 + c, rows : 2 * rows, cols : 2 * cols]
        parts = [spread[(3 * kind + c) * rows : (3 * kind + c + 1) * rows] for kind in range(3)]
        total = parts[0] + 2.0 * pic * parts[1] + aim * parts[2] + 1.6 * (pic - aim)
        for side in range(2):
            part = total[side * SEGMENTS : (side + 1) * SEGMENTS]
            skewed = pltpu.roll(part, 0, 1, stride=TILE_SIDE, stride_axis=0)
            for tile in range(TILES_DEV):
                moved = pltpu.roll(skewed, HALF - TILE_SIDE * tile, 1) if tile else skewed
                kept = jnp.where(lane_row == seg_at, moved, 0.0)
                out_ref[tile, c : c + 1, side * HALF : (side + 1) * HALF] = jnp.sum(
                    kept, axis=0, keepdims=True
                )


def ssim_pull(place, wide):
    return pl.pallas_call(
        ssim_kernel,
        out_shape=jax.ShapeDtypeStruct((TILES_DEV, 8, TILE_SIDE * TILE_SIDE), jnp.float32),
        in_specs=[smem(), vmem()],
        out_specs=vmem(),
        scratch_shapes=[pltpu.VMEM((12 * wide.shape[1], wide.shape[2]), jnp.float32)],
        name="ssim_pull",
    )(place, wide)


def body(splats, sh_coeffs, send_list, block_slots, block_tiles, target):
    row_band = lax.axis_index("gauss")
    col_band = lax.axis_index("tile")
    owners = lax.axis_size("gauss")
    peers = lax.axis_size("tile")
    own_records = jnp.concatenate([splats[0:6], shade(splats[6:9], sh_coeffs)], axis=0)
    received = lax.all_to_all(
        own_records[:, send_list], "gauss", split_axis=1, concat_axis=1, tiled=True
    )
    tile_ids = block_tiles[0]
    slot_rows = block_slots[0]
    slots_total = slot_rows.shape[0]
    live = jnp.sum((tile_ids < TILES_DEV).astype(jnp.int32))
    info = jnp.stack([live, TILE_SIDE * TILES_DEV * col_band, TILE_SIDE * row_band]).astype(jnp.int32)
    pairs = (
        slot_rows.reshape(slots_total, SEGMENTS, STEPS)
        .transpose(0, 2, 1)
        .reshape(slots_total // 2, 2 * BLOCK)
    )
    rendered, recs, saved = draw_tiles(tile_ids, info, received, pairs, slots_total)
    rows_here, cols_here = rendered.shape[1:]
    place = jnp.stack(
        [row_band * rows_here, col_band * cols_here, rows_here * owners, cols_here * peers]
    ).astype(jnp.int32)
    tile_grad = ssim_pull(place, exchange(rendered, target))
    table_grad = pull_tiles(tile_ids, info, recs, saved, tile_grad, pairs, received.shape[1])
    back_records = lax.all_to_all(table_grad, "gauss", split_axis=1, concat_axis=1, tiled=True)
    own_grad = jnp.zeros_like(own_records).at[:, send_list].set(back_records)
    unused_colour, shade_pull = jax.vjp(shade, splats[6:9], sh_coeffs)
    dir_grad, grad_sh = shade_pull(own_grad[6:9])
    grad_splats = jnp.concatenate([own_grad[0:6], dir_grad], axis=0)
    return (rendered, grad_splats, grad_sh)


def solution(mesh):
    in_specs = (
        P(None, ("gauss", "tile")),
        P(None, ("gauss", "tile")),
        P(("gauss", "tile")),
        P("gauss", "tile", None),
        P("gauss", "tile"),
        P(None, "gauss", "tile"),
    )
    out_specs = (P(None, "gauss", "tile"), P(None, ("gauss", "tile")), P(None, ("gauss", "tile")))
    return jax.shard_map(body, mesh=mesh, in_specs=in_specs, out_specs=out_specs, check_vma=False)
```

```python
import functools
import math

import jax
import jax.numpy as jnp
from jax import lax
from jax.experimental import pallas as pl
from jax.experimental.pallas import tpu as pltpu
from jax.sharding import PartitionSpec as P

TILE_SIDE = 16
TILES_DEV = 8


HIGHEST = lax.Precision.HIGHEST
BASE_ZERO = 0.28209479177387814
BASE_ONE = 0.4886025119029199
BASE_TWO = (
    1.0925484305920792,
    -1.0925484305920792,
    0.31539156525252005,
    -1.0925484305920792,
    0.5462742152960396,
)
BASE_THREE = (
    -0.5900435899266435,
    2.890611442640554,
    -0.4570457994644658,
    0.3731763325901154,
    -0.4570457994644658,
    1.445305721320277,
    -0.5900435899266435,
)
CONST_ONE = 0.0001
CONST_TWO = 0.0009


def harmonics(direction):
    coord_x, coord_y, coord_z = (direction[0], direction[1], direction[2])
    square_x, square_y, square_z = (coord_x * coord_x, coord_y * coord_y, coord_z * coord_z)
    rows_list = [
        jnp.full_like(coord_x, BASE_ZERO),
        -BASE_ONE * coord_y,
        BASE_ONE * coord_z,
        -BASE_ONE * coord_x,
        BASE_TWO[0] * coord_x * coord_y,
        BASE_TWO[1] * coord_y * coord_z,
        BASE_TWO[2] * (2.0 * square_z - square_x - square_y),
        BASE_TWO[3] * coord_x * coord_z,
        BASE_TWO[4] * (square_x - square_y),
        BASE_THREE[0] * coord_y * (3.0 * square_x - square_y),
        BASE_THREE[1] * coord_x * coord_y * coord_z,
        BASE_THREE[2] * coord_y * (4.0 * square_z - square_x - square_y),
        BASE_THREE[3] * coord_z * (2.0 * square_z - 3.0 * square_x - 3.0 * square_y),
        BASE_THREE[4] * coord_x * (4.0 * square_z - square_x - square_y),
        BASE_THREE[5] * coord_z * (square_x - square_y),
        BASE_THREE[6] * coord_x * (square_x - 3.0 * square_y),
    ]
    return jnp.stack(rows_list)


def shade(direction, coeffs):
    basis = harmonics(direction)
    return 0.5 + jnp.sum(coeffs.reshape(3, 16, -1) * basis[None], axis=1)


SEGMENTS = 8
STEPS = 16
BLOCK = SEGMENTS * STEPS
HALF = 128
CENTRE = 7.5
CHUNK = 256


def selector(slots_row, base, rows):
    rows_at = lax.broadcasted_iota(jnp.int32, (rows, slots_row.shape[1]), 0) + base
    return jnp.where(rows_at == slots_row, 1.0, 0.0).astype(jnp.bfloat16)


def halves(value):
    high = value.astype(jnp.bfloat16)
    low = (value - high.astype(jnp.float32)).astype(jnp.bfloat16)
    return high, low


def pixel_axes():
    lanes = lax.broadcasted_iota(jnp.int32, (SEGMENTS, HALF), 1)
    along = (lanes % TILE_SIDE).astype(jnp.float32) - CENTRE
    down = (lanes // TILE_SIDE).astype(jnp.float32) - CENTRE
    return along, (down, down + float(HALF // TILE_SIDE))


def thirds(value):
    first = value.astype(jnp.bfloat16)
    rest = value - first.astype(jnp.float32)
    second = rest.astype(jnp.bfloat16)
    third = (rest - second.astype(jnp.float32)).astype(jnp.bfloat16)
    return first, second, third


def fill_widener(wide_ref):
    rows_at = lax.broadcasted_iota(jnp.int32, wide_ref.shape, 0) % 16
    field_at = lax.broadcasted_iota(jnp.int32, wide_ref.shape, 1) // HALF
    wide_ref[...] = jnp.where(rows_at == field_at, 1.0, 0.0).astype(jnp.bfloat16)


def widen(rec, wide_ref, column_ref):
    column_ref[...] = lax.dot_general(
        jnp.concatenate(thirds(rec), axis=0),
        wide_ref[...],
        (((0,), (0,)), ((), ())),
        preferred_element_type=jnp.float32,
    )


def columns_of(col_ref, step):
    rows = slice(step * SEGMENTS, (step + 1) * SEGMENTS)
    return [col_ref[rows, k * HALF : (k + 1) * HALF] for k in range(9)]


def alphas_of(cols, along, down):
    delta_x = along - cols[0]
    delta_y = down - cols[1]
    exponent = cols[2] * delta_x * delta_x + delta_y * (cols[3] * delta_x + cols[4] * delta_y)
    return cols[5] * jnp.exp(exponent)


def forward_kernel(
    tile_ref, info_ref, recv_ref, slots_ref, picture_ref, rec_ref, saved_ref,
    pad_ref, split_ref, col_ref, image_ref, wide_ref,
):
    live = info_ref[0]
    own = recv_ref.shape[1]
    pad_ref[...] = jnp.zeros_like(pad_ref)
    pad_ref[0:9, :] = recv_ref[...]
    for at, part in enumerate(thirds(pad_ref[...])):
        split_ref[16 * at : 16 * (at + 1), :] = part
    fill_widener(wide_ref)
    row_at = lax.broadcasted_iota(jnp.int32, (16, BLOCK), 0)
    base_y = info_ref[2].astype(jnp.float32) + CENTRE

    def collect(pair, carry):
        slots_row = slots_ref[pl.ds(pair, 1), :]
        found = jnp.zeros((48, 2 * BLOCK), jnp.float32)
        for base in range(0, own, CHUNK):
            found = found + jnp.dot(
                split_ref[:, base : base + CHUNK],
                selector(slots_row, base, CHUNK),
                preferred_element_type=jnp.float32,
            )
        joined = found[0:16] + found[16:32] + found[32:48]
        for side in range(2):
            slot = 2 * pair + side
            rec = joined[:, side * BLOCK : (side + 1) * BLOCK]
            tile = jnp.minimum(tile_ref[slot], TILES_DEV - 1)
            base_x = (info_ref[1] + TILE_SIDE * tile).astype(jnp.float32) + CENTRE
            shift = jnp.where(row_at == 0, base_x, jnp.where(row_at == 1, base_y, 0.0))
            scale = jnp.where(
                row_at == 3, -1.0, jnp.where((row_at == 2) | (row_at == 4), -0.5, 1.0)
            )
            shown = jnp.where(row_at == 5, 1.0 / (1.0 + jnp.exp(-rec)), (rec - shift) * scale)
            rec_ref[slot] = shown
        return carry

    lax.fori_loop(0, (live + 1) // 2, collect, 0)
    along, downs = pixel_axes()
    seg_at = lax.broadcasted_iota(jnp.int32, (SEGMENTS, HALF), 0)

    def draw_local(slot, column_ref):
        widen(rec_ref[slot], wide_ref, column_ref)
        through = [jnp.ones((SEGMENTS, HALF), jnp.float32) for side in range(2)]
        sums = [[jnp.zeros((SEGMENTS, HALF), jnp.float32) for c in range(3)] for side in range(2)]
        for step in range(STEPS):
            cols = columns_of(column_ref, step)
            for side in range(2):
                weight = alphas_of(cols, along, downs[side]) * through[side]
                through[side] = through[side] - weight
                for c in range(3):
                    sums[side][c] = sums[side][c] + cols[6 + c] * weight
        return through, sums

    def draw_join(slot, carry, through, sums):
        tile = tile_ref[slot]
        fresh = (slot == 0) | (tile != tile_ref[jnp.maximum(slot - 1, 0)])
        after = []
        for side in range(2):
            start = jnp.where(fresh, 1.0, carry[side])
            running = through[side]
            for shift in (1, 2, 4):
                running = jnp.where(
                    seg_at >= shift, running * pltpu.roll(running, shift, 0), running
                )
            before = jnp.where(seg_at == 0, 1.0, pltpu.roll(running, 1, 0)) * start
            after.append(start * running[SEGMENTS - 1 : SEGMENTS])
            lanes = slice(side * HALF, (side + 1) * HALF)
            saved_ref[slot, 0, :, lanes] = before
            saved_ref[slot, 1, :, lanes] = through[side]
            for c in range(3):
                saved_ref[slot, 2 + c, :, lanes] = sums[side][c]
                shade_sum = jnp.sum(before * sums[side][c], axis=0, keepdims=True)
                held = jnp.where(fresh, 0.0, image_ref[tile, c : c + 1, lanes])
                image_ref[tile, c : c + 1, lanes] = held + shade_sum
        return tuple(after)

    def draw(pair, carry):
        locals_two = [draw_local(2 * pair + k, col_ref.at[k]) for k in range(2)]
        for k in range(2):
            carry = draw_join(2 * pair + k, carry, *locals_two[k])
        return carry

    ones = jnp.ones((1, HALF), jnp.float32)
    lax.fori_loop(0, (live + 1) // 2, draw, (ones, ones))
    lane_tile = lax.broadcasted_iota(jnp.int32, (SEGMENTS, HALF), 1) // TILE_SIDE
    for side in range(2):
        lanes = slice(side * HALF, (side + 1) * HALF)
        for c in range(3):
            shown = jnp.zeros((SEGMENTS, HALF), jnp.float32)
            for tile in range(TILES_DEV):
                row = jnp.broadcast_to(image_ref[tile, c : c + 1, lanes], (SEGMENTS, HALF))
                moved = pltpu.roll(row, TILE_SIDE * tile, 1) if tile else row
                for bit in (1, 2, 4):
                    moved = jnp.where(
                        (seg_at & bit) > 0, pltpu.roll(moved, HALF - TILE_SIDE * bit, 1), moved
                    )
                shown = jnp.where(lane_tile == tile, moved, shown)
            picture_ref[c, side * SEGMENTS : (side + 1) * SEGMENTS, :] = shown


def backward_kernel(
    tile_ref, info_ref, rec_ref, saved_ref, grad_ref, slots_ref, out_ref,
    col_ref, weight_ref, pull_ref, block_ref, acc_ref, wide_ref,
):
    live = info_ref[0]
    own = out_ref.shape[1]
    slots_total = rec_ref.shape[0]
    block_ref[...] = jnp.zeros_like(block_ref)
    acc_ref[...] = jnp.zeros_like(acc_ref)
    fill_widener(wide_ref)
    along, downs = pixel_axes()
    seg_at = lax.broadcasted_iota(jnp.int32, (SEGMENTS, HALF), 0)
    rows16 = lax.broadcasted_iota(jnp.int32, (16, 2 * HALF), 0)
    pixels = lax.broadcasted_iota(jnp.int32, (16, 2 * HALF), 1)
    wide_u = (pixels % TILE_SIDE).astype(jnp.float32) - CENTRE
    wide_v = (pixels // TILE_SIDE).astype(jnp.float32) - CENTRE
    basis = jnp.zeros((16, 2 * HALF), jnp.float32)
    for at, term in enumerate(
        (jnp.ones_like(wide_u), wide_u, wide_v, wide_u * wide_u, wide_u * wide_v, wide_v * wide_v)
    ):
        basis = jnp.where(rows16 == at, term, basis)
    basis = basis.astype(jnp.bfloat16)
    across = (((1,), (1,)), ((), ()))

    def pull_one(slot, carry, column_ref, heavy_ref, force_ref):
        tile = tile_ref[slot]
        used = tile < TILES_DEV
        final = (slot >= live - 1) | (tile != tile_ref[jnp.minimum(slot + 1, slots_total - 1)])
        rec = rec_ref[slot]
        widen(rec, wide_ref, column_ref)
        grads = grad_ref[jnp.minimum(tile, TILES_DEV - 1)]
        after = []
        behind = []
        through = []
        colour_g = []
        for side in range(2):
            lanes = slice(side * HALF, (side + 1) * HALF)
            start = jnp.where(final, 0.0, carry[side])
            tints = [jnp.broadcast_to(grads[c : c + 1, lanes], (SEGMENTS, HALF)) for c in range(3)]
            colour_g.append(tints)
            total = tints[0] * saved_ref[slot, 2, :, lanes]
            for c in (1, 2):
                total = total + tints[c] * saved_ref[slot, 2 + c, :, lanes]
            factor = saved_ref[slot, 1, :, lanes]
            for shift in (1, 2, 4):
                inside = seg_at < SEGMENTS - shift
                total = jnp.where(
                    inside, total + factor * pltpu.roll(total, SEGMENTS - shift, 0), total
                )
                factor = jnp.where(
                    inside, factor * pltpu.roll(factor, SEGMENTS - shift, 0), factor
                )
            entering = total + factor * start
            after.append(entering[0:1])
            behind.append(
                jnp.where(seg_at < SEGMENTS - 1, pltpu.roll(entering, SEGMENTS - 1, 0), start)
            )
            through.append(saved_ref[slot, 0, :, lanes])
        alphas = [[], []]
        weights = [[], []]
        for step in range(STEPS):
            cols = columns_of(column_ref, step)
            for side in range(2):
                alpha = alphas_of(cols, along, downs[side])
                weight = alpha * through[side]
                through[side] = through[side] - weight
                alphas[side].append(alpha)
                weights[side].append(weight)
                lanes = slice(side * HALF, (side + 1) * HALF)
                heavy_ref[step * SEGMENTS : (step + 1) * SEGMENTS, lanes] = weight
        for step in reversed(range(STEPS)):
            cols = columns_of(column_ref, step)
            for side in range(2):
                lanes = slice(side * HALF, (side + 1) * HALF)
                tints = colour_g[side]
                lit = tints[0] * cols[6] + tints[1] * cols[7] + tints[2] * cols[8]
                gap = lit - behind[side]
                behind[side] = behind[side] + alphas[side][step] * gap
                force_ref[step * SEGMENTS : (step + 1) * SEGMENTS, lanes] = (
                    weights[side][step] * gap
                )
        found = lax.dot_general(
            basis,
            jnp.concatenate(halves(force_ref[...]), axis=0),
            across,
            preferred_element_type=jnp.float32,
        )
        moment = found[:, :BLOCK] + found[:, BLOCK:]
        painted = lax.dot_general(
            jnp.concatenate(halves(grads), axis=0),
            jnp.concatenate(halves(heavy_ref[...]), axis=0),
            across,
            preferred_element_type=jnp.float32,
        )
        painted = painted[0:8] + painted[8:16]
        painted = painted[:, :BLOCK] + painted[:, BLOCK:]
        m_0, m_x, m_y, m_xx, m_xy, m_yy = [moment[k : k + 1] for k in range(6)]
        at_x, at_y, con_a, con_b, con_c, open_s = [rec[k : k + 1] for k in range(6)]
        h_x = m_x - at_x * m_0
        h_y = m_y - at_y * m_0
        h_xx = m_xx - 2.0 * at_x * m_x + at_x * at_x * m_0
        h_xy = m_xy - at_x * m_y - at_y * m_x + at_x * at_y * m_0
        h_yy = m_yy - 2.0 * at_y * m_y + at_y * at_y * m_0
        block_ref[slot, 0:1, :] = jnp.where(used, -2.0 * con_a * h_x - con_b * h_y, 0.0)
        block_ref[slot, 1:2, :] = jnp.where(used, -2.0 * con_c * h_y - con_b * h_x, 0.0)
        block_ref[slot, 2:3, :] = jnp.where(used, -0.5 * h_xx, 0.0)
        block_ref[slot, 3:4, :] = jnp.where(used, -h_xy, 0.0)
        block_ref[slot, 4:5, :] = jnp.where(used, -0.5 * h_yy, 0.0)
        block_ref[slot, 5:6, :] = jnp.where(used, (1.0 - open_s) * m_0, 0.0)
        block_ref[slot, 6:9, :] = jnp.where(used, painted[0:3], 0.0)
        return tuple(after)

    def pull(turn, carry):
        pair = (live + 1) // 2 - 1 - turn
        for k in (1, 0):
            carry = pull_one(2 * pair + k, carry, col_ref.at[k], weight_ref.at[k], pull_ref.at[k])
        return carry

    zeros = jnp.zeros((1, HALF), jnp.float32)
    lax.fori_loop(0, (live + 1) // 2, pull, (zeros, zeros))

    def spread(pair, carry):
        slots_row = slots_ref[pl.ds(pair, 1), :]
        both = jnp.concatenate([block_ref[2 * pair], block_ref[2 * pair + 1]], axis=1)
        parts = jnp.concatenate(halves(both), axis=0)
        for base in range(0, own, CHUNK):
            lanes = slice(base, base + CHUNK)
            acc_ref[:, lanes] += lax.dot_general(
                parts, selector(slots_row, base, CHUNK), across, preferred_element_type=jnp.float32
            )
        return carry

    lax.fori_loop(0, (live + 1) // 2, spread, 0)
    out_ref[...] = acc_ref[0:9, :] + acc_ref[16:25, :]


def pick_kernel(table_ref, list_ref, out_ref, pad_ref, split_ref):
    own = table_ref.shape[1]
    pad_ref[...] = jnp.zeros_like(pad_ref)
    pad_ref[0:9, :] = table_ref[...]
    for at, part in enumerate(thirds(pad_ref[...])):
        split_ref[16 * at : 16 * (at + 1), :] = part

    def one(turn, carry):
        lanes = pl.ds(pl.multiple_of(turn * CHUNK, CHUNK), CHUNK)
        wanted = list_ref[:, lanes]
        found = jnp.zeros((48, CHUNK), jnp.float32)
        for base in range(0, own, CHUNK):
            found = found + jnp.dot(
                split_ref[:, base : base + CHUNK],
                selector(wanted, base, CHUNK),
                preferred_element_type=jnp.float32,
            )
        out_ref[:, lanes] = (found[0:16] + found[16:32] + found[32:48])[0:9]
        return carry

    lax.fori_loop(0, own // CHUNK, one, 0)


def place_kernel(table_ref, list_ref, out_ref, pad_ref, acc_ref):
    own = table_ref.shape[1]
    pad_ref[...] = jnp.zeros_like(pad_ref)
    pad_ref[0:9, :] = table_ref[...]
    acc_ref[...] = jnp.zeros_like(acc_ref)

    def one(turn, carry):
        lanes = pl.ds(pl.multiple_of(turn * CHUNK, CHUNK), CHUNK)
        wanted = list_ref[:, lanes]
        parts = jnp.concatenate(thirds(pad_ref[:, lanes]), axis=0)
        for base in range(0, own, CHUNK):
            acc_ref[:, base : base + CHUNK] += lax.dot_general(
                parts,
                selector(wanted, base, CHUNK),
                (((1,), (1,)), ((), ())),
                preferred_element_type=jnp.float32,
            )
        return carry

    lax.fori_loop(0, own // CHUNK, one, 0)
    out_ref[...] = acc_ref[0:9, :] + acc_ref[16:25, :] + acc_ref[32:41, :]


def permuted(kernel, table, listed, scratch_type, name):
    own = table.shape[1]
    return pl.pallas_call(
        kernel,
        out_shape=jax.ShapeDtypeStruct(table.shape, jnp.float32),
        in_specs=[vmem(), vmem()],
        out_specs=vmem(),
        scratch_shapes=[pltpu.VMEM((16, own), jnp.float32), pltpu.VMEM((48, own), scratch_type)],
        name=name,
    )(table, listed.reshape(1, own))


def smem():
    return pl.BlockSpec(memory_space=pltpu.SMEM)


def vmem():
    return pl.BlockSpec(memory_space=pltpu.VMEM)


def draw_tiles(tile_ids, info, received, pairs, slots_total):
    own = received.shape[1]
    side = TILE_SIDE * TILE_SIDE
    return pl.pallas_call(
        forward_kernel,
        out_shape=(
            jax.ShapeDtypeStruct((3, TILE_SIDE, TILES_DEV * TILE_SIDE), jnp.float32),
            jax.ShapeDtypeStruct((slots_total, 16, BLOCK), jnp.float32),
            jax.ShapeDtypeStruct((slots_total, 5, SEGMENTS, side), jnp.float32),
        ),
        in_specs=[smem(), smem(), vmem(), vmem()],
        out_specs=(vmem(), vmem(), vmem()),
        scratch_shapes=[
            pltpu.VMEM((16, own), jnp.float32),
            pltpu.VMEM((48, own), jnp.bfloat16),
            pltpu.VMEM((2, BLOCK, 9 * HALF), jnp.float32),
            pltpu.VMEM((TILES_DEV + 1, 8, side), jnp.float32),
            pltpu.VMEM((48, 9 * HALF), jnp.bfloat16),
        ],
        name="draw_tiles",
    )(tile_ids, info, received, pairs)


def pull_tiles(tile_ids, info, recs, saved, grads, pairs, own):
    slots_total = recs.shape[0]
    side = TILE_SIDE * TILE_SIDE
    return pl.pallas_call(
        backward_kernel,
        out_shape=jax.ShapeDtypeStruct((9, own), jnp.float32),
        in_specs=[smem(), smem(), vmem(), vmem(), vmem(), vmem()],
        out_specs=vmem(),
        scratch_shapes=[
            pltpu.VMEM((2, BLOCK, 9 * HALF), jnp.float32),
            pltpu.VMEM((2, BLOCK, side), jnp.float32),
            pltpu.VMEM((2, BLOCK, side), jnp.float32),
            pltpu.VMEM((slots_total, 16, BLOCK), jnp.float32),
            pltpu.VMEM((32, own), jnp.float32),
            pltpu.VMEM((48, 9 * HALF), jnp.bfloat16),
        ],
        name="pull_tiles",
    )(tile_ids, info, recs, saved, grads, pairs)


WAYS = [(down, right) for down in (-1, 0, 1) for right in (-1, 0, 1) if (down, right) != (0, 0)]
NORM = sum(math.exp(-m * m / 4.5) for m in range(-5, 6))


def halo_kernel(bands, cols_total, shown_ref, target_ref, out_ref, send_sem, recv_sem):
    band = lax.axis_index("gauss")
    column = lax.axis_index("tile")
    rows, cols = shown_ref.shape[1:]
    out_ref[...] = jnp.zeros_like(out_ref)
    barrier = pltpu.get_barrier_semaphore()

    def exists(way):
        there_band = band + way[0]
        there_col = column + way[1]
        return (
            (there_band >= 0) & (there_band < bands) & (there_col >= 0) & (there_col < cols_total)
        )

    def copies(at):
        down, right = WAYS[at]
        landing = len(WAYS) - 1 - at
        return [
            pltpu.make_async_remote_copy(
                src_ref=source,
                dst_ref=out_ref.at[
                    pl.ds(3 * kind, 3), pl.ds(rows * (1 - down), rows), pl.ds(cols * (1 - right), cols)
                ],
                send_sem=send_sem.at[kind, at],
                recv_sem=recv_sem.at[kind, landing],
                device_id=(band + down, column + right),
                device_id_type=pl.DeviceIdType.MESH,
            )
            for kind, source in enumerate((shown_ref, target_ref))
        ]

    for at, way in enumerate(WAYS):

        @pl.when(exists(way))
        def _(way=way):
            pl.semaphore_signal(
                barrier,
                inc=1,
                device_id=(band + way[0], column + way[1]),
                device_id_type=pl.DeviceIdType.MESH,
            )

    peers = sum(exists(way).astype(jnp.int32) for way in WAYS)
    pl.semaphore_wait(barrier, peers)

    for at, way in enumerate(WAYS):

        @pl.when(exists(way))
        def _(at=at):
            for copy in copies(at):
                copy.start()

    out_ref[0:3, rows : 2 * rows, cols : 2 * cols] = shown_ref[...]
    out_ref[3:6, rows : 2 * rows, cols : 2 * cols] = target_ref[...]
    for at, way in enumerate(WAYS):

        @pl.when(exists(way))
        def _(at=at):
            for copy in copies(at):
                copy.wait_send()
            for kind, source in enumerate((shown_ref, target_ref)):
                pltpu.make_async_remote_copy(
                    src_ref=source,
                    dst_ref=out_ref.at[
                        pl.ds(3 * kind, 3),
                        pl.ds(rows * (1 + WAYS[at][0]), rows),
                        pl.ds(cols * (1 + WAYS[at][1]), cols),
                    ],
                    send_sem=send_sem.at[kind, at],
                    recv_sem=recv_sem.at[kind, at],
                    device_id=(band + WAYS[at][0], column + WAYS[at][1]),
                    device_id_type=pl.DeviceIdType.MESH,
                ).wait_recv()


def exchange(rendered, target):
    channels, rows, cols = rendered.shape
    return pl.pallas_call(
        functools.partial(halo_kernel, lax.axis_size("gauss"), lax.axis_size("tile")),
        out_shape=jax.ShapeDtypeStruct((2 * channels, 3 * rows, 3 * cols), jnp.float32),
        in_specs=[vmem(), vmem()],
        out_specs=vmem(),
        scratch_shapes=[
            pltpu.SemaphoreType.DMA((2, len(WAYS))),
            pltpu.SemaphoreType.DMA((2, len(WAYS))),
        ],
        compiler_params=pltpu.CompilerParams(collective_id=0, has_side_effects=True),
        name="halo",
    )(rendered, target)


def banded(shape, offset):
    gap = (
        lax.broadcasted_iota(jnp.int32, shape, 0) - lax.broadcasted_iota(jnp.int32, shape, 1) + offset
    ).astype(jnp.float32)
    return jnp.where(jnp.abs(gap) < 5.5, jnp.exp(gap * gap / -4.5) * (1.0 / NORM), 0.0)


def exact_dot(left, right):
    return jnp.dot(left, right, precision=HIGHEST, preferred_element_type=jnp.float32)


def ssim_kernel(place_ref, wide_ref, out_ref, stack_ref):
    tall, wide = wide_ref.shape[1:]
    rows, cols = tall // 3, wide // 3
    row_from, rows_mid = rows // 2, 2 * rows
    col_from, cols_mid = cols // 2, 2 * cols
    for c in range(3):
        pic = wide_ref[c]
        aim = wide_ref[3 + c]
        for kind, plane in enumerate((pic, aim, pic * pic + aim * aim, pic * aim)):
            at = 3 * kind + c
            stack_ref[at * tall : (at + 1) * tall, :] = plane
    across = exact_dot(stack_ref[...], banded((wide, cols_mid), -col_from))
    moments = exact_dot(
        banded((rows_mid, tall), row_from),
        jnp.concatenate([across[at * tall : (at + 1) * tall] for at in range(12)], axis=1),
    )
    row_at = place_ref[0] + row_from - rows + lax.broadcasted_iota(jnp.int32, (rows_mid, cols_mid), 0)
    col_at = place_ref[1] + col_from - cols + lax.broadcasted_iota(jnp.int32, (rows_mid, cols_mid), 1)
    inside = (row_at >= 0) & (row_at < place_ref[2]) & (col_at >= 0) & (col_at < place_ref[3])
    slopes = [None] * 9
    for c in range(3):
        mu_x, mu_y, squares, cross = [
            moments[:, (3 * kind + c) * cols_mid : (3 * kind + c + 1) * cols_mid] for kind in range(4)
        ]
        mean_xy = mu_x * mu_y
        mean_sq = mu_x * mu_x + mu_y * mu_y
        top_1 = 2.0 * mean_xy + CONST_ONE
        top_2 = 2.0 * (cross - mean_xy) + CONST_TWO
        low_1 = mean_sq + CONST_ONE
        low_2 = squares - mean_sq + CONST_TWO
        inverse = -0.2 / (low_1 * low_2)
        value = top_1 * top_2 * inverse
        value_1 = value * low_2 * inverse * -5.0
        value_2 = value * low_1 * inverse * -5.0
        slope_mean = 2.0 * mu_y * (top_2 - top_1) * inverse - 2.0 * mu_x * (value_1 - value_2)
        for kind, slope in enumerate((slope_mean, -value_2, 2.0 * top_1 * inverse)):
            slopes[3 * kind + c] = jnp.where(inside, slope, 0.0)
    down = exact_dot(
        banded((rows, rows_mid), rows - row_from), jnp.concatenate(slopes, axis=1)
    )
    spread = exact_dot(
        jnp.concatenate([down[:, at * cols_mid : (at + 1) * cols_mid] for at in range(9)], axis=0),
        banded((cols_mid, cols), col_from - cols),
    )
    lane_row = lax.broadcasted_iota(jnp.int32, (SEGMENTS, HALF), 1) // TILE_SIDE
    seg_at = lax.broadcasted_iota(jnp.int32, (SEGMENTS, HALF), 0)
    out_ref[...] = jnp.zeros_like(out_ref)
    for c in range(3):
        pic = wide_ref[c, rows : 2 * rows, cols : 2 * cols]
        aim = wide_ref[3 + c, rows : 2 * rows, cols : 2 * cols]
        parts = [spread[(3 * kind + c) * rows : (3 * kind + c + 1) * rows] for kind in range(3)]
        total = parts[0] + 2.0 * pic * parts[1] + aim * parts[2] + 1.6 * (pic - aim)
        for side in range(2):
            part = total[side * SEGMENTS : (side + 1) * SEGMENTS]
            skewed = pltpu.roll(part, 0, 1, stride=TILE_SIDE, stride_axis=0)
            for tile in range(TILES_DEV):
                moved = pltpu.roll(skewed, HALF - TILE_SIDE * tile, 1) if tile else skewed
                kept = jnp.where(lane_row == seg_at, moved, 0.0)
                out_ref[tile, c : c + 1, side * HALF : (side + 1) * HALF] = jnp.sum(
                    kept, axis=0, keepdims=True
                )


def ssim_pull(place, wide):
    return pl.pallas_call(
        ssim_kernel,
        out_shape=jax.ShapeDtypeStruct((TILES_DEV, 8, TILE_SIDE * TILE_SIDE), jnp.float32),
        in_specs=[smem(), vmem()],
        out_specs=vmem(),
        scratch_shapes=[pltpu.VMEM((12 * wide.shape[1], wide.shape[2]), jnp.float32)],
        name="ssim_pull",
    )(place, wide)


def body(splats, sh_coeffs, send_list, block_slots, block_tiles, target):
    row_band = lax.axis_index("gauss")
    col_band = lax.axis_index("tile")
    owners = lax.axis_size("gauss")
    peers = lax.axis_size("tile")
    own_records = jnp.concatenate([splats[0:6], shade(splats[6:9], sh_coeffs)], axis=0)
    received = lax.all_to_all(
        permuted(pick_kernel, own_records, send_list, jnp.bfloat16, "pick"), "gauss", split_axis=1, concat_axis=1, tiled=True
    )
    tile_ids = block_tiles[0]
    slot_rows = block_slots[0]
    slots_total = slot_rows.shape[0]
    live = jnp.sum((tile_ids < TILES_DEV).astype(jnp.int32))
    info = jnp.stack([live, TILE_SIDE * TILES_DEV * col_band, TILE_SIDE * row_band]).astype(jnp.int32)
    pairs = (
        slot_rows.reshape(slots_total, SEGMENTS, STEPS)
        .transpose(0, 2, 1)
        .reshape(slots_total // 2, 2 * BLOCK)
    )
    rendered, recs, saved = draw_tiles(tile_ids, info, received, pairs, slots_total)
    rows_here, cols_here = rendered.shape[1:]
    place = jnp.stack(
        [row_band * rows_here, col_band * cols_here, rows_here * owners, cols_here * peers]
    ).astype(jnp.int32)
    tile_grad = ssim_pull(place, exchange(rendered, target))
    table_grad = pull_tiles(tile_ids, info, recs, saved, tile_grad, pairs, received.shape[1])
    back_records = lax.all_to_all(table_grad, "gauss", split_axis=1, concat_axis=1, tiled=True)
    own_grad = permuted(place_kernel, back_records, send_list, jnp.float32, "place")
    unused_colour, shade_pull = jax.vjp(shade, splats[6:9], sh_coeffs)
    dir_grad, grad_sh = shade_pull(own_grad[6:9])
    grad_splats = jnp.concatenate([own_grad[0:6], dir_grad], axis=0)
    return (rendered, grad_splats, grad_sh)


def solution(mesh):
    in_specs = (
        P(None, ("gauss", "tile")),
        P(None, ("gauss", "tile")),
        P(("gauss", "tile")),
        P("gauss", "tile", None),
        P("gauss", "tile"),
        P(None, "gauss", "tile"),
    )
    out_specs = (P(None, "gauss", "tile"), P(None, ("gauss", "tile")), P(None, ("gauss", "tile")))
    return jax.shard_map(body, mesh=mesh, in_specs=in_specs, out_specs=out_specs, check_vma=False)
```
